256 devices in a mesh: ctx: 64 (over y, z, core), head: 4 (over x).
Axes of the slice: x: 4, y: 4, z: 8, core: 2. Of those that a mesh axis runs over, the one named last changes fastest.
Arguments:
- query_in: bfloat16 [8192, 2048], P('ctx', 'head'), may hold values from -6 to 6
- key_in: bfloat16 [8192, 2048], P('ctx', 'head'), may hold values from -6 to 6
- value_in: bfloat16 [8192, 4096], P('ctx', 'head'), may hold values from -6 to 6
- gate_in: bfloat16 [8192, 4096], P('ctx', 'head'), may hold values from -6 to 6
- conv_query: float32 [4, 2048], P(None, 'head'), may hold values from -3 to 3
- conv_key: float32 [4, 2048], P(None, 'head'), may hold values from -3 to 3
- conv_value: float32 [4, 4096], P(None, 'head'), may hold values from -3 to 3
- decay_in: float32 [32, 8192], P('head', 'ctx'), may hold values from -14 to 0.1
- beta_in: float32 [32, 8192], P('head', 'ctx'), may hold values from -2.5 to -1.5
- norm_gain: float32 [128], replicated, may hold values from 0.5 to 1.5
- doc_lengths: int32 [128], replicated, may hold values from 1 to 2048, 8192 in all
- out_weight: bfloat16 [4096, 2048], P('head'), may hold values from -0.09375 to 0.09375
Outputs:
- projected: bfloat16 [2048, 8192], P('head', 'ctx')
The draws below stay inside these ranges and needn't reach their ends.
Inputs may be any that keep to these rules, and one draw needn't show every extreme that they name: `doc_lengths`: lengths of the 128 packed documents in packing order; they sum to 8192, and the longest has exactly 2048 tokens.
All inputs are finite; a program needn't handle non-finite values.
Results may differ from the reference program's by a relative error of at most 0.017.
Values may be sent and summed in bfloat16 or wider, within the bound.
A program may use at most 192 MiB of HBM per device.

```python
import math
import jax
import jax.numpy as jnp
import numpy as np
from jax import lax

D = 2048
VALUE_HEAD_COUNT = 32
HK = 16
DK = 128
DV = 128
KW = 4
SPAN = 64
TOKENS_PER_SHARD = 128
PACKED_TOKENS = 8192
DOCS = 128
MOST_DOC = 2048
N_HEAD = 4


def draw_decay_in(key, part):
    random_subkeys = jax.random.split(key, 5)
    slow_heads = jax.random.bernoulli(random_subkeys[0], 0.5, (VALUE_HEAD_COUNT, 1))
    block_count = PACKED_TOKENS // TOKENS_PER_SHARD
    block_scale = jnp.exp(jax.random.uniform(random_subkeys[1], (VALUE_HEAD_COUNT, block_count, 1), jnp.float32, -0.7, 0.7))
    block_scale = jnp.broadcast_to(block_scale, (VALUE_HEAD_COUNT, block_count, TOKENS_PER_SHARD)).reshape(VALUE_HEAD_COUNT, PACKED_TOKENS)
    token_scale = jnp.exp(jax.random.uniform(random_subkeys[2], (VALUE_HEAD_COUNT, PACKED_TOKENS), jnp.float32, -0.7, 0.7))
    base_rate = jnp.where(slow_heads, 0.25 / MOST_DOC, 1.0 / 40.0)
    frequency = base_rate * block_scale * token_scale
    sudden_spike = jax.random.bernoulli(random_subkeys[3], 4.0 / PACKED_TOKENS, (VALUE_HEAD_COUNT, PACKED_TOKENS))
    spike_frequency = jax.random.uniform(random_subkeys[4], (VALUE_HEAD_COUNT, PACKED_TOKENS), jnp.float32, 0.25, 0.7)
    frequency = jnp.where(sudden_spike, spike_frequency, frequency)
    return jnp.log(jnp.expm1(frequency)).astype(jnp.float32)


def draw_key_in(key, part):
    random_subkeys = jax.random.split(key, 3)
    width = HK * DK
    signs = jnp.where(jax.random.bernoulli(random_subkeys[0], 0.5, (1, width)), 1.0, -1.0)
    offset = signs * jax.random.uniform(random_subkeys[1], (1, width), jnp.float32, 0.5, 2.5)
    noise = jax.random.normal(random_subkeys[2], (PACKED_TOKENS, width), jnp.float32)
    return jnp.clip(offset + noise, -6.0, 6.0).astype(jnp.bfloat16)


def steps_of(key, extent, cuts, least, largest):
    factor_of, own = 1.0, jax.random.fold_in(key, 6)
    for position, parts in cuts:
        steps = jnp.exp(jax.random.uniform(jax.random.fold_in(own, position), (parts,), jnp.float32, least / len(cuts), largest / len(cuts)))
        factor_of = factor_of * jnp.repeat(steps, extent[position] // parts).reshape([-1 if axis == position else 1 for axis in range(len(extent))])
    return factor_of


def length_profile(amount, total, most, lean):
    portions = [(1 << 20) // math.isqrt(rank ** lean) + 1 for rank in range(2, amount + 1)]
    spare, holding = total - most - (amount - 1), [1] * (amount - 1)
    while spare > 0:
        candidates = [i for i in range(amount - 1) if holding[i] < most]
        whole, remaining = sum([portions[i] for i in candidates]), spare
        for i in candidates:
            addition = min(most - holding[i], max(1, remaining * portions[i] // whole), spare)
            holding[i] = holding[i] + addition
            spare = spare - addition
    return np.array([most] + holding)


def uneven(key, count, total, bound, lean):
    if count == 2:
        one = jax.random.randint(key, (), max(1, total - bound), min(bound, total - 1) + 1)
        return jnp.stack([one, total - one])
    tallies = jnp.asarray(length_profile(count, total, bound, lean), jnp.int32)
    twos = (count - 1) // 2
    giver, taker = tallies[1:1 + 2 * twos:2], tallies[2:2 + 2 * twos:2]
    room = jnp.minimum(giver - 1, bound - taker)
    shifted = jax.random.randint(jax.random.fold_in(key, 1), (twos,), 0, 1 << 20) % (room + 1)
    tallies = tallies.at[1:1 + 2 * twos:2].set(giver - shifted).at[2:2 + 2 * twos:2].set(taker + shifted)
    return tallies[jax.random.permutation(jax.random.fold_in(key, 2), count)]


def normal_values(own_key, dims, scale, bound, cuts=(), kind=jnp.bfloat16):
    loudness = steps_of(own_key, dims, cuts, -0.22, 0.18) if cuts else 1.0
    values = jax.random.normal(own_key, dims, jnp.float32) * scale * loudness
    return jnp.minimum(jnp.maximum(values, -bound), bound).astype(kind)


def setup_inputs(seed: int = 0) -> dict:
    key_of = jax.random.split(jax.random.key(seed), 13)
    query_in = normal_values(key_of[0], (PACKED_TOKENS, HK * DK), 1.0, 6.0, ((0, 64), (1, 4)))
    key_in = draw_key_in(jax.random.fold_in(key_of[12], 71), 0)
    value_in = normal_values(key_of[2], (PACKED_TOKENS, VALUE_HEAD_COUNT * DV), 1.0, 6.0, ((0, 64), (1, 4)))
    gate_in = normal_values(key_of[3], (PACKED_TOKENS, VALUE_HEAD_COUNT * DV), 1.0, 6.0, ((0, 64), (1, 4)))
    conv_query = normal_values(key_of[4], (KW, HK * DK), KW ** -0.5, 3.0, ((1, 4),), jnp.float32)
    conv_key = normal_values(key_of[5], (KW, HK * DK), KW ** -0.5, 3.0, ((1, 4),), jnp.float32)
    conv_value = normal_values(key_of[6], (KW, VALUE_HEAD_COUNT * DV), KW ** -0.5, 3.0, ((1, 4),), jnp.float32)
    decay_in = draw_decay_in(jax.random.fold_in(key_of[12], 71), 0)
    beta_in = jnp.clip(-2.5 + 1.0 * jax.random.uniform(key_of[8], (VALUE_HEAD_COUNT, PACKED_TOKENS), jnp.float32) ** steps_of(key_of[8], (VALUE_HEAD_COUNT, PACKED_TOKENS), ((0, 4), (1, 64)), -0.2, 0.2), -2.5, -1.5)
    norm_gain = jnp.clip(1.0 + 0.1 * jax.random.normal(key_of[9], (DV,), jnp.float32), 0.5, 1.5)
    doc_lengths = uneven(key_of[10], DOCS, PACKED_TOKENS, MOST_DOC, 2).astype(jnp.int32)
    out_weight = normal_values(key_of[11], (VALUE_HEAD_COUNT * DV, D), (VALUE_HEAD_COUNT * DV) ** -0.5, 0.09375, ((0, 4),))
    return {"query_in": query_in, "key_in": key_in, "value_in": value_in, "gate_in": gate_in, "conv_query": conv_query, "conv_key": conv_key, "conv_value": conv_value, "decay_in": decay_in, "beta_in": beta_in, "norm_gain": norm_gain, "doc_lengths": doc_lengths, "out_weight": out_weight}


PRECISE = lax.Precision.HIGHEST

def shard_conv(before, current, weight, keep_masks):
    margin = weight.shape[0] - 1
    count_rows = current.shape[0]
    padded = jnp.concatenate([before, current], axis=0).astype(jnp.float32)
    summed = jnp.zeros((count_rows, current.shape[1]), jnp.float32)
    for offset in range(margin + 1):
        summed = summed + weight[offset][None, :] * padded[offset:offset + count_rows] * keep_masks[margin - offset][:, None]
    return jax.nn.silu(summed)

def unit_heads(vectors, head_count):
    reshaped = vectors.reshape(vectors.shape[0], head_count, -1)
    return reshaped / jnp.sqrt(lax.optimization_barrier(jnp.sum(reshaped * reshaped, axis=-1, keepdims=True)) + 1e-06)

def span_terms(queries, keys_unit, values, log_gamma, beta_values, resets):
    length = resets.shape[0]
    segment = jnp.cumsum(resets).astype(jnp.int32)
    cumulative = jnp.cumsum(log_gamma, axis=-1)
    row_index = jnp.arange(length, dtype=jnp.int32)[:, None]
    col_index = jnp.arange(length, dtype=jnp.int32)[None, :]
    same_doc = (segment[:, None] == segment[None, :]) & (row_index >= col_index)
    strict = same_doc & (row_index > col_index)
    log_ratio = cumulative[:, :, None] - cumulative[:, None, :]
    decay_pairs = jnp.exp(jnp.where(same_doc[None], log_ratio, -1e+30))
    key_gram = jnp.einsum('hid,hjd->hij', keys_unit, keys_unit, precision=PRECISE)
    lower_part = jnp.where(strict[None], beta_values[:, :, None] * key_gram * decay_pairs, 0.0)
    head_start = jnp.where(segment[None, :] == 0, jnp.exp(cumulative), 0.0)
    last_segment = segment[length - 1]
    to_end = jnp.where(segment[None, :] == last_segment, jnp.exp(cumulative[:, length - 1:] - cumulative), 0.0)
    through = jnp.where(last_segment == 0, jnp.exp(cumulative[:, length - 1]), 0.0)
    values_in = lax.linalg.triangular_solve(lower_part, beta_values[:, :, None] * values, left_side=True, lower=True, unit_diagonal=True)
    keys_in = lax.linalg.triangular_solve(lower_part, (beta_values * head_start)[:, :, None] * keys_unit, left_side=True, lower=True, unit_diagonal=True)
    scores = jnp.einsum('hid,hjd->hij', queries, keys_unit, precision=PRECISE)
    inside = jnp.where(same_doc[None], scores * decay_pairs, 0.0)
    return (values_in, keys_in, inside, head_start, to_end, through)

def reference(query_in, key_in, value_in, gate_in, conv_query, conv_key, conv_value, decay_in, beta_in, norm_gain, doc_lengths, out_weight):
    margin = KW - 1
    positions = jnp.arange(PACKED_TOKENS, dtype=jnp.int32)
    doc_starts = (jnp.cumsum(doc_lengths) - doc_lengths).astype(jnp.int32)
    start_flags = jnp.any(positions[:, None] == doc_starts[None, :], axis=1).astype(jnp.int32)
    running = jnp.concatenate([jnp.zeros((margin,), jnp.int32), jnp.cumsum(start_flags).astype(jnp.int32)])
    padded_query = jnp.concatenate([jnp.zeros((margin, HK * DK), jnp.bfloat16), query_in], axis=0)
    padded_key = jnp.concatenate([jnp.zeros((margin, HK * DK), jnp.bfloat16), key_in], axis=0)
    padded_value = jnp.concatenate([jnp.zeros((margin, VALUE_HEAD_COUNT * DV), jnp.bfloat16), value_in], axis=0)
    log_gamma = -jax.nn.softplus(decay_in)
    beta_values = jax.nn.sigmoid(beta_in)
    group_ratio = VALUE_HEAD_COUNT // HK

    def span_step(carried, span_index):
        first_row = (span_index * SPAN).astype(jnp.int32)

        def window(array):
            return lax.dynamic_slice_in_dim(array, first_row, SPAN + margin, 0)
        counts_here = window(running)
        keep_masks = [(counts_here[margin:] - counts_here[margin - lag_steps:margin - lag_steps + SPAN] == 0).astype(jnp.float32) for lag_steps in range(margin + 1)]
        resets = lax.dynamic_slice_in_dim(start_flags, first_row, SPAN, 0)
        rows_query = window(padded_query)
        rows_key = window(padded_key)
        rows_value = window(padded_value)
        queries = unit_heads(shard_conv(rows_query[:margin], rows_query[margin:], conv_query, keep_masks), HK)
        keys_unit = unit_heads(shard_conv(rows_key[:margin], rows_key[margin:], conv_key, keep_masks), HK)
        values = shard_conv(rows_value[:margin], rows_value[margin:], conv_value, keep_masks).reshape(SPAN, VALUE_HEAD_COUNT, DV)
        queries = jnp.repeat(queries, group_ratio, axis=1).transpose(1, 0, 2)
        keys_unit = jnp.repeat(keys_unit, group_ratio, axis=1).transpose(1, 0, 2)
        values = values.transpose(1, 0, 2)
        gamma_part = lax.dynamic_slice_in_dim(log_gamma, first_row, SPAN, 1)
        beta_part = lax.dynamic_slice_in_dim(beta_values, first_row, SPAN, 1)
        values_in, keys_in, inside, head_start, to_end, through = span_terms(queries, keys_unit, values, gamma_part, beta_part, resets)
        fresh_values = values_in - jnp.einsum('hcd,hde->hce', keys_in, carried, precision=PRECISE)
        result = jnp.einsum('hcd,hde->hce', queries * head_start[..., None], carried, precision=PRECISE) + jnp.einsum('hij,hje->hie', inside, fresh_values, precision=PRECISE)
        carried = through[:, None, None] * carried + jnp.einsum('hcd,hce->hde', keys_unit * to_end[..., None], fresh_values, precision=PRECISE)
        heads_out = result.transpose(1, 0, 2)
        gate_values = lax.dynamic_slice_in_dim(gate_in, first_row, SPAN, 0).astype(jnp.float32).reshape(SPAN, VALUE_HEAD_COUNT, DV)
        normed = heads_out / jnp.sqrt(lax.optimization_barrier(jnp.mean(heads_out * heads_out, axis=-1, keepdims=True)) + 1e-06) * norm_gain * jax.nn.silu(gate_values)
        return (carried, normed.reshape(SPAN, VALUE_HEAD_COUNT * DV).astype(jnp.bfloat16))
    zeros_state = jnp.zeros((VALUE_HEAD_COUNT, DK, DV), jnp.float32)
    _, mixed_blocks = lax.scan(span_step, zeros_state, jnp.arange(PACKED_TOKENS // SPAN, dtype=jnp.int32))
    mixed_rows = mixed_blocks.reshape(PACKED_TOKENS, VALUE_HEAD_COUNT * DV)
    group_cols = VALUE_HEAD_COUNT * DV // N_HEAD
    summed = jnp.zeros((PACKED_TOKENS, D), jnp.float32)
    for group_index in range(N_HEAD):
        low = group_index * group_cols
        partial_value = jnp.dot(mixed_rows[:, low:low + group_cols].astype(jnp.float32), out_weight[low:low + group_cols].astype(jnp.float32), preferred_element_type=jnp.float32).astype(jnp.bfloat16)
        partial_value = lax.optimization_barrier(partial_value)
        summed = summed + partial_value.astype(jnp.float32)
    return summed.T.astype(jnp.bfloat16)
```

```python
import jax
import jax.numpy as jnp
from jax import lax
from jax.experimental import pallas as pl
from jax.experimental.pallas import tpu as pltpu
from jax.sharding import PartitionSpec as P

MESH = pl.DeviceIdType.MESH
F32, BF16 = jnp.float32, jnp.bfloat16
DK = 128
ROWS = 128
TOK = 256
HALO = 16
CHIPS = 8
OWN = 4


def dot(a, b):
    return jnp.dot(a, b, preferred_element_type=F32)


def kernel(
    q_hbm, k_hbm, v_hbm, g_hbm, dec_hbm, beta_hbm, w_hbm,
    cq_ref, ck_ref, cv_ref, docs_ref, gain_ref,
    out_ref,
    qx, kx, vx, gx, dx, bx, xf, w_vm,
    mb, qeff, oloc, rbuf, q8, s0buf, sout, sbuf, mx, mixfull, sendp, recvp,
    lsem, xs, xr, hs, hr, as_, ar, ys, yr, ss, sr, ms, mr, ps, pr,
):
    ctx, x = lax.axis_index("ctx"), lax.axis_index("head")
    n_ctx, n_x = lax.axis_size("ctx"), lax.axis_size("head")
    c = lax.rem(ctx, 2)
    chip = ctx // 2
    z = lax.rem(chip, CHIPS)
    line = ctx - 2 * z - c
    n_chips = n_ctx // 2
    partner = chip * 2 + 1 - c
    prev_tail = lax.rem(chip + n_chips - 1, n_chips) * 2 + 1
    next_head = lax.rem(chip + 1, n_chips) * 2
    own = z // OWN == c
    head_at = z - OWN * c
    up = lax.rem(ctx + 2 * CHIPS, n_ctx)
    down = lax.rem(ctx + n_ctx - 2 * CHIPS, n_ctx)

    def at(chip_z):
        return line + 2 * chip_z + c

    w_copy = pltpu.make_async_copy(w_hbm, w_vm, lsem.at[0])
    w_copy.start()
    cols = lambda core, width: pl.ds(pl.multiple_of(core * width, 128), width)
    mine = pl.ds(pl.multiple_of(HALO + ROWS * c, 16), ROWS)
    gmine = pl.ds(pl.multiple_of(ROWS * c, 16), ROWS)
    local = []
    for n, (src, dst) in enumerate((
        (q_hbm.at[:, cols(c, 256)], qx.at[mine]),
        (k_hbm.at[:, cols(c, 256)], kx.at[mine]),
        (v_hbm.at[:, cols(c, 512)], vx.at[mine]),
        (g_hbm.at[:, cols(c, 512)], gx.at[gmine]),
        (dec_hbm, dx.at[c]),
        (beta_hbm, bx.at[c]),
    )):
        local.append(pltpu.make_async_copy(src, dst, lsem.at[n + 1]))
        local[-1].start()

    barrier = pltpu.get_barrier_semaphore()

    def greet(**device):
        pl.semaphore_signal(barrier, inc=1, device_id=device, device_id_type=MESH)

    greet(ctx=partner)
    greet(ctx=prev_tail)
    for k in range(1, 4):
        greet(head=lax.rem(x + k, n_x))
    for i in range(OWN):
        owner = OWN * c + i

        @pl.when(z != owner)
        def _():
            greet(ctx=at(owner))

    @pl.when(own)
    def _():
        greet(ctx=down)
        for k in range(1, CHIPS):
            greet(ctx=at(lax.rem(z + k, CHIPS)))

    expect = 1 + 2 * c + 3 + jnp.where(own, OWN - 1 + CHIPS - 1 + 1, OWN)
    pl.semaphore_wait(barrier, expect)

    tail = pl.ds(ROWS - HALO, HALO)
    front = pl.ds(0, HALO)
    halo = []
    for core in range(2):
        for n, (src, dst, width) in enumerate(((q_hbm, qx, 256), (k_hbm, kx, 256), (v_hbm, vx, 512))):
            halo.append(pltpu.make_async_remote_copy(
                src.at[tail, pl.ds(core * width, width)], dst.at[front],
                hs.at[core, n], hr.at[n], device_id={"ctx": next_head + core}, device_id_type=MESH,
            ))

    @pl.when(c == 1)
    def _():
        for copy in halo:
            copy.start()

    trade = []
    for n, (src, dst) in enumerate((
        (dec_hbm, dx.at[c]),
        (beta_hbm, bx.at[c]),
        (k_hbm.at[:, cols(1 - c, 256)], kx.at[mine]),
        (q_hbm.at[:, cols(1 - c, 256)], qx.at[mine]),
        (v_hbm.at[:, cols(1 - c, 512)], vx.at[mine]),
        (g_hbm.at[:, cols(1 - c, 512)], gx.at[gmine]),
    )):
        trade.append(pltpu.make_async_remote_copy(
            src, dst, xs.at[n], xr.at[n], device_id={"ctx": partner}, device_id_type=MESH,
        ))
        trade[-1].start()

    first = chip * TOK
    sub = lax.broadcasted_iota(jnp.int32, (128, 128), 0)
    lane = lax.broadcasted_iota(jnp.int32, (128, 128), 1)
    lens = jnp.broadcast_to(docs_ref[...].astype(F32), (128, 128))
    starts_col = jnp.sum(jnp.where(lane < sub, lens, 0.0), axis=1, keepdims=True)
    starts_row = jnp.sum(jnp.where(sub < lane, lens.T, 0.0), axis=0, keepdims=True)
    pos_row = (first + lax.broadcasted_iota(jnp.int32, (128, TOK), 1)).astype(F32)
    seg_row = jnp.sum(jnp.where(starts_col <= pos_row, 1.0, 0.0), axis=0, keepdims=True)
    seg_prev = jnp.sum(jnp.where(starts_col <= (first - 1).astype(F32), 1.0, 0.0), axis=0, keepdims=True)
    seg_end = jnp.sum(jnp.where(starts_col <= (first + TOK - 1).astype(F32), 1.0, 0.0), axis=0, keepdims=True)
    pos_col = first + lax.broadcasted_iota(jnp.int32, (TOK, 128), 0)

    def seg_at(back):
        return jnp.sum(jnp.where(starts_row <= (pos_col - back).astype(F32), 1.0, 0.0), axis=1, keepdims=True)

    seg_col = seg_at(0)
    keeps = [None] + [(seg_at(j) == seg_col).astype(F32) for j in range(1, 4)]
    row_i = lax.broadcasted_iota(jnp.int32, (TOK, TOK), 0)
    col_i = lax.broadcasted_iota(jnp.int32, (TOK, TOK), 1)
    same_doc = (seg_col == seg_row) & (row_i >= col_i)
    eye = (row_i == col_i).astype(F32)
    upper = (row_i <= col_i).astype(F32)

    for copy in local:
        copy.wait()
    for copy in trade:
        copy.wait_recv()

    decay = jnp.concatenate([dx[0], dx[1]], axis=1)
    log_gamma = -jax.nn.softplus(decay)
    cum8 = jnp.dot(log_gamma, upper, precision=lax.Precision.HIGHEST, preferred_element_type=F32)
    beta8 = jax.nn.sigmoid(jnp.concatenate([bx[0], bx[1]], axis=1))
    pick = lambda rows: jnp.where(c == 0, rows[:OWN], rows[OWN:])
    cum, beta = pick(cum8), pick(beta8)
    last = cum[:, TOK - 1:]
    to_end = jnp.where(seg_row == seg_end, jnp.exp(last - cum), 0.0)
    through = jnp.where(seg_end == seg_prev, jnp.exp(last), 0.0)
    by_token = jnp.concatenate([cum, beta], axis=0).T
    in_first = seg_col == seg_prev

    for n in range(3):
        halo[n].wait_recv()

    for ref, lo, width in ((qx, 0, 256), (kx, 256, 256), (vx, 512, 512)):
        xf[:, lo:lo + width] = ref[...].astype(F32)

    def conv(w_ref, lo, width):
        taps = w_ref[:, cols(c, width)]
        total = None
        for i in range(4):
            term = taps[i:i + 1] * xf[HALO - 3 + i:HALO - 3 + i + TOK, lo:lo + width]
            if i < 3:
                term = term * keeps[3 - i]
            total = term if total is None else total + term
        return total * jax.nn.sigmoid(total)

    def unit(rows):
        return rows * lax.rsqrt(jnp.sum(rows * rows, axis=-1, keepdims=True) + 1e-6)

    q_all, k_all = conv(cq_ref, 0, 256), conv(ck_ref, 256, 256)
    v_all = conv(cv_ref, 512, 512)

    block = lambda size: (row_i // size) == (col_i // size)
    cuts = [block(16)]
    for size in (16, 32, 64, 128):
        cuts.append(block(2 * size) & ~block(size) if size < 128 else ~block(size))

    sends = []
    for kh in range(2):
        kf = unit(k_all[:, kh * DK:(kh + 1) * DK])
        qf = unit(q_all[:, kh * DK:(kh + 1) * DK])
        kb, qb = kf.astype(BF16), qf.astype(BF16)
        k_t = kf.T
        k_tb = k_t.astype(BF16)
        gram = dot(kb, k_tb)
        scores = dot(qb, k_tb)
        for i in (2 * kh, 2 * kh + 1):
            cum_col = by_token[:, i:i + 1]
            beta_col = by_token[:, OWN + i:OWN + i + 1]
            start_col = jnp.where(in_first, jnp.exp(cum_col), 0.0)
            pairs = jnp.exp(jnp.where(same_doc, cum_col - cum[i:i + 1], -1e30))
            low = jnp.where(row_i > col_i, beta_col * gram * pairs, 0.0)
            inside = (scores * pairs).astype(BF16)
            n1f = jnp.where(cuts[0], -low, 0.0)
            n1 = n1f.astype(BF16)
            n2 = dot(n1, n1).astype(BF16)
            n4 = dot(n2, n2).astype(BF16)
            n8 = dot(n4, n4).astype(BF16)
            t = eye + n1f
            for power in (n2, n4, n8):
                t = t + dot(t.astype(BF16), power)
            for cut in cuts[1:]:
                edge = jnp.where(cut, low, 0.0).astype(BF16)
                tb = t.astype(BF16)
                t = t - dot(tb, dot(edge, tb).astype(BF16))
            v = v_all[:, i * DK:(i + 1) * DK]
            rhs = jnp.concatenate([beta_col * v, (beta_col * start_col) * kf], axis=1).astype(BF16)
            uw = dot(t.astype(BF16), rhs).astype(BF16)
            k_end = (k_t * to_end[i:i + 1]).astype(BF16)
            kuw = dot(k_end, uw)
            iuw = dot(inside, uw)
            mb[i, :, :DK] = (through[i:i + 1] * eye[:DK, :DK] - kuw[:, DK:]).astype(BF16)
            mb[i, :, DK:] = kuw[:, :DK].astype(BF16)
            owner = OWN * c + i
            send = pltpu.make_async_remote_copy(
                mb.at[i], rbuf.at[z], as_.at[i], ar.at[z], device_id={"ctx": at(owner)}, device_id_type=MESH,
            )
            sends.append((owner, send))

            @pl.when(z != owner)
            def _():
                send.start()

            @pl.when(z == owner)
            def _():
                rbuf[z] = mb[i]

            oloc[i] = iuw[:, :DK]
            qeff[i] = (qf * start_col - iuw[:, DK:]).astype(BF16)

    back = []
    for j in range(CHIPS):
        back.append(pltpu.make_async_remote_copy(
            sout.at[j], sbuf.at[jnp.where(own, head_at, 0)], ss.at[j], sr.at[jnp.where(own, head_at, 0)],
            device_id={"ctx": at(j)}, device_id_type=MESH,
        ))
    ahead = pltpu.make_async_remote_copy(q8, s0buf, ys, yr, device_id={"ctx": up}, device_id_type=MESH)

    @pl.when(own)
    def _():
        for j in range(CHIPS):
            @pl.when(z != j)
            def _():
                pltpu.make_async_remote_copy(
                    mb.at[0], rbuf.at[j], as_.at[0], ar.at[j], device_id={"ctx": at(j)}, device_id_type=MESH,
                ).wait_recv()

        def then(later, earlier):
            joined = dot(later[:, :DK], earlier)
            return jnp.concatenate([joined[:, :DK], joined[:, DK:] + later[:, DK:].astype(F32)], axis=1).astype(BF16)

        one = [rbuf[j] for j in range(CHIPS)]
        two = [then(one[2 * j + 1], one[2 * j]) for j in range(4)]
        four = [then(two[1], two[0]), then(two[3], two[2])]
        q8[...] = (dot(four[1][:, :DK], four[0][:, DK:]) + four[1][:, DK:].astype(F32)).astype(BF16)
        ahead.start()
        six = then(two[2], four[0])
        pre = [None, one[0], two[0], then(one[2], two[0]), four[0], then(one[4], four[0]), six, then(one[6], six)]
        ahead.wait_recv()
        s0 = jnp.where(ctx >= 2 * CHIPS, s0buf[...].astype(F32), 0.0).astype(BF16)
        for j in (4, 3, 5, 2, 6, 1, 7, 0):
            if j == 0:
                state = s0
            else:
                state = (dot(pre[j][:, :DK], s0) + pre[j][:, DK:].astype(F32)).astype(BF16)
            sout[j] = state

            @pl.when(z != j)
            def _():
                back[j].start()

            @pl.when(z == j)
            def _():
                sbuf[head_at] = state

    swaps = []
    for i in range(OWN):
        @pl.when(z != OWN * c + i)
        def _():
            pltpu.make_async_remote_copy(
                sout.at[0], sbuf.at[i], ss.at[0], sr.at[i], device_id={"ctx": partner}, device_id_type=MESH,
            ).wait_recv()

        o = oloc[i] + dot(qeff[i], sbuf[i])
        gate = gx[:, i * DK:(i + 1) * DK].astype(F32)
        normed = o * lax.rsqrt(jnp.mean(o * o, axis=-1, keepdims=True) + 1e-6)
        mx[:, i * DK:(i + 1) * DK] = (normed * gain_ref[...] * (gate * jax.nn.sigmoid(gate))).astype(BF16)
        here = cols(OWN * c + i, DK)
        swaps.append(pltpu.make_async_remote_copy(
            mx.at[pl.ds(pl.multiple_of(ROWS * (1 - c), 16), ROWS), pl.ds(i * DK, DK)], mixfull.at[:, here],
            ms.at[i], mr.at[i], device_id={"ctx": partner}, device_id_type=MESH,
        ))
        swaps[-1].start()
        mixfull[:, here] = mx[gmine, i * DK:(i + 1) * DK]
    for swap in swaps:
        swap.wait_recv()
    w_copy.wait()

    mixed = mixfull[...]
    width = w_vm.shape[1] // 4
    parts = []
    for k in (2, 1, 3):
        to = lax.rem(x + k, n_x)
        sendp[k - 1] = dot(mixed, w_vm[:, cols(to, width)]).astype(BF16)
        parts.append(pltpu.make_async_remote_copy(
            sendp.at[k - 1], recvp.at[k - 1], ps.at[k - 1], pr.at[k - 1], device_id={"head": to}, device_id_type=MESH,
        ))
        parts[-1].start()
    total = dot(mixed, w_vm[:, cols(x, width)]).astype(BF16).astype(F32)
    for part, k in zip(parts, (2, 1, 3)):
        part.wait_recv()
        total = total + recvp[k - 1].astype(F32)
    out_ref[...] = total.T.astype(BF16)

    for copy in trade + swaps + parts:
        copy.wait_send()

    @pl.when(c == 1)
    def _():
        for copy in halo:
            copy.wait_send()

    for owner, send in sends:
        @pl.when(z != owner)
        def _():
            send.wait_send()

    @pl.when(own)
    def _():
        ahead.wait_send()
        for j in range(CHIPS):
            @pl.when(z != j)
            def _():
                back[j].wait_send()


def body(
    query_in, key_in, value_in, gate_in, conv_query, conv_key, conv_value,
    decay_in, beta_in, norm_gain, doc_lengths, out_weight,
):
    anywhere, vmem = pl.BlockSpec(memory_space=pl.ANY), pl.BlockSpec(memory_space=pltpu.VMEM)
    dma = pltpu.SemaphoreType.DMA
    features = out_weight.shape[1] // 4
    return pl.pallas_call(
        kernel,
        out_shape=jax.ShapeDtypeStruct((features, ROWS), BF16),
        in_specs=[anywhere] * 7 + [vmem] * 5,
        out_specs=vmem,
        scratch_shapes=[
            pltpu.VMEM((HALO + TOK, 256), BF16),
            pltpu.VMEM((HALO + TOK, 256), BF16),
            pltpu.VMEM((HALO + TOK, 512), BF16),
            pltpu.VMEM((TOK, 512), BF16),
            pltpu.VMEM((2, 8, ROWS), F32),
            pltpu.VMEM((2, 8, ROWS), F32),
            pltpu.VMEM((HALO + TOK, 1024), F32),
            pltpu.VMEM(out_weight.shape, BF16),
            pltpu.VMEM((OWN, DK, 2 * DK), BF16),
            pltpu.VMEM((OWN, TOK, DK), BF16),
            pltpu.VMEM((OWN, TOK, DK), F32),
            pltpu.VMEM((CHIPS, DK, 2 * DK), BF16),
            pltpu.VMEM((DK, DK), BF16),
            pltpu.VMEM((DK, DK), BF16),
            pltpu.VMEM((CHIPS, DK, DK), BF16),
            pltpu.VMEM((OWN, DK, DK), BF16),
            pltpu.VMEM((TOK, OWN * DK), BF16),
            pltpu.VMEM((ROWS, 2 * OWN * DK), BF16),
            pltpu.VMEM((3, ROWS, features), BF16),
            pltpu.VMEM((3, ROWS, features), BF16),
            dma((7,)), dma((6,)), dma((6,)), dma((2, 3)), dma((3,)),
            dma((OWN,)), dma((CHIPS,)), dma, dma, dma((CHIPS,)), dma((OWN,)),
            dma((OWN,)), dma((OWN,)), dma((3,)), dma((3,)),
        ],
        compiler_params=pltpu.CompilerParams(
            collective_id=0, has_side_effects=True, vmem_limit_bytes=56 << 20
        ),
        name="mixer",
    )(
        query_in, key_in, value_in, gate_in, decay_in, beta_in, out_weight,
        conv_query, conv_key, conv_value, doc_lengths.reshape(1, -1), norm_gain.reshape(1, -1),
    )


def solution(mesh):
    return jax.shard_map(
        body,
        mesh=mesh,
        in_specs=(
            P("ctx", "head"), P("ctx", "head"), P("ctx", "head"), P("ctx", "head"),
            P(None, "head"), P(None, "head"), P(None, "head"),
            P("head", "ctx"), P("head", "ctx"), P(), P(), P("head", None),
        ),
        out_specs=P("head", "ctx"),
        check_vma=False,
    )
```

```python
import jax
import jax.numpy as jnp
from jax import lax
from jax.experimental import pallas as pl
from jax.experimental.pallas import tpu as pltpu
from jax.sharding import PartitionSpec as P

MESH = pl.DeviceIdType.MESH
F32, BF16 = jnp.float32, jnp.bfloat16
DK = 128
ROWS = 128
TOK = 256
HALO = 16
CHIPS = 8
OWN = 4


def dot(a, b):
    return jnp.dot(a, b, preferred_element_type=F32)


def kernel(
    q_hbm, k_hbm, v_hbm, g_hbm, dec_hbm, beta_hbm, w_hbm,
    cq_ref, ck_ref, cv_ref, docs_ref, gain_ref,
    out_ref,
    qx, kx, vx, gx, dx, bx, hb, hx, xf, act, w_vm,
    mb, qeff, oloc, rbuf, pre, q8, s0buf, sout, sbuf, gated, mx, mixfull, own_part, sendp, recvp,
    lsem, xs, xr, hl, hs, hr, as_, ar, ys, yr, ss, sr, ms, mr, ps, pr, told,
):
    ctx, x = lax.axis_index("ctx"), lax.axis_index("head")
    n_ctx, n_x = lax.axis_size("ctx"), lax.axis_size("head")
    c = lax.rem(ctx, 2)
    chip = ctx // 2
    z = lax.rem(chip, CHIPS)
    line = ctx - 2 * z - c
    n_chips = n_ctx // 2
    partner = chip * 2 + 1 - c
    prev_tail = jnp.maximum(chip - 1, 0) * 2 + 1
    next_head = jnp.minimum(chip + 1, n_chips - 1) * 2
    has_prev, has_next = chip > 0, chip < n_chips - 1
    sends_halo = (c == 1) & has_next
    own = z // OWN == c
    head_at = z - OWN * c
    has_up, has_down = ctx < n_ctx - 2 * CHIPS, ctx >= 2 * CHIPS
    up = jnp.minimum(ctx + 2 * CHIPS, n_ctx - 1)
    down = jnp.maximum(ctx - 2 * CHIPS, 0)

    def at(chip_z):
        return line + 2 * chip_z + c

    w_copy = pltpu.make_async_copy(w_hbm, w_vm, lsem.at[0])
    w_copy.start()
    cols = lambda core, width: pl.ds(pl.multiple_of(core * width, 128), width)
    mine = pl.ds(pl.multiple_of(ROWS * c, 16), ROWS)
    local = []
    for n, (src, dst) in enumerate((
        (q_hbm.at[:, cols(c, 256)], qx.at[mine]),
        (k_hbm.at[:, cols(c, 256)], kx.at[mine]),
        (v_hbm.at[:, cols(c, 512)], vx.at[mine]),
        (g_hbm.at[:, cols(c, 512)], gx.at[mine]),
        (dec_hbm, dx.at[c]),
        (beta_hbm, bx.at[c]),
    )):
        local.append(pltpu.make_async_copy(src, dst, lsem.at[n + 1]))
        local[-1].start()

    pack = []
    for core in range(2):
        for n, (src, lo, width) in enumerate(((q_hbm, 0, 256), (k_hbm, 256, 256), (v_hbm, 512, 512))):
            pack.append(pltpu.make_async_copy(
                src.at[pl.ds(ROWS - HALO, HALO), pl.ds(core * width, width)],
                hb.at[core, :, pl.ds(lo, width)], hl.at[core, n],
            ))

    @pl.when(sends_halo)
    def _():
        for copy in pack:
            copy.start()

    @pl.when(chip == 0)
    def _():
        hx[...] = jnp.zeros_like(hx)

    @pl.when(~has_down)
    def _():
        s0buf[...] = jnp.zeros_like(s0buf)

    barrier = pltpu.get_barrier_semaphore()

    def signal(sem, **device):
        pl.semaphore_signal(sem, inc=1, device_id=device, device_id_type=MESH)

    def ring(k):
        return at(lax.rem(z + k + CHIPS, CHIPS))

    x_next, x_prev = lax.rem(x + 1, n_x), lax.rem(x + n_x - 1, n_x)
    signal(barrier, ctx=partner)
    signal(barrier, head=x_next)
    signal(barrier, head=x_prev)
    signal(barrier, ctx=ring(1))
    signal(barrier, ctx=ring(-1))

    @pl.when(has_prev)
    def _():
        signal(barrier, ctx=prev_tail)

    @pl.when(has_down)
    def _():
        signal(barrier, ctx=down)

    pl.semaphore_wait(barrier, 5 + jnp.where(sends_halo, 2, 0) + jnp.where(has_up, 1, 0))

    halo = []
    for core in range(2):
        halo.append(pltpu.make_async_remote_copy(
            hb.at[core], hx, hs.at[core], hr, device_id={"ctx": next_head + core}, device_id_type=MESH,
        ))

    @pl.when(sends_halo)
    def _():
        for copy in pack:
            copy.wait()
        for copy in halo:
            copy.start()

    trade = []
    for n, (src, dst) in enumerate((
        (dec_hbm, dx.at[c]),
        (beta_hbm, bx.at[c]),
        (k_hbm.at[:, cols(1 - c, 256)], kx.at[mine]),
        (q_hbm.at[:, cols(1 - c, 256)], qx.at[mine]),
        (v_hbm.at[:, cols(1 - c, 512)], vx.at[mine]),
        (g_hbm.at[:, cols(1 - c, 512)], gx.at[mine]),
    )):
        trade.append(pltpu.make_async_remote_copy(
            src, dst, xs.at[n], xr.at[n], device_id={"ctx": partner}, device_id_type=MESH,
        ))
        trade[-1].start()

    signal(told.at[0], ctx=ring(1))
    signal(told.at[1], ctx=ring(-1))
    signal(told.at[2], head=x_next)

    first = chip * TOK
    sub = lax.broadcasted_iota(jnp.int32, (128, 128), 0)
    lane = lax.broadcasted_iota(jnp.int32, (128, 128), 1)
    lens = jnp.broadcast_to(docs_ref[...].astype(F32), (128, 128))
    starts_col = jnp.sum(jnp.where(lane < sub, lens, 0.0), axis=1, keepdims=True)
    starts_row = jnp.sum(jnp.where(sub < lane, lens.T, 0.0), axis=0, keepdims=True)
    pos_row = (first + lax.broadcasted_iota(jnp.int32, (128, TOK), 1)).astype(F32)
    seg_row = jnp.sum(jnp.where(starts_col <= pos_row, 1.0, 0.0), axis=0, keepdims=True)
    seg_prev = jnp.sum(jnp.where(starts_col <= (first - 1).astype(F32), 1.0, 0.0), axis=0, keepdims=True)
    seg_end = jnp.sum(jnp.where(starts_col <= (first + TOK - 1).astype(F32), 1.0, 0.0), axis=0, keepdims=True)
    pos_col = first + lax.broadcasted_iota(jnp.int32, (TOK, 128), 0)

    def seg_at(back):
        return jnp.sum(jnp.where(starts_row <= (pos_col - back).astype(F32), 1.0, 0.0), axis=1, keepdims=True)

    seg_col = seg_at(0)
    keeps = [None] + [(seg_at(j) == seg_col).astype(F32) for j in range(1, 4)]
    upper = (lax.broadcasted_iota(jnp.int32, (TOK, TOK), 0) <= lax.broadcasted_iota(jnp.int32, (TOK, TOK), 1)).astype(F32)
    halves = (slice(0, 128), slice(128, 256))
    quads = ((0, 0), (1, 0), (1, 1))
    same_doc = {}
    for r, s in quads:
        same = seg_col[halves[r]] == seg_row[:, halves[s]]
        same_doc[r, s] = same & (sub >= lane) if r == s else same

    for copy in local:
        copy.wait()
    for copy in trade[:5]:
        copy.wait_recv()

    pl.semaphore_wait(told.at[0], 1)
    pl.semaphore_wait(told.at[1], 1)
    signal(told.at[3], ctx=ring(2))
    signal(told.at[4], ctx=ring(-2))

    decay = jnp.concatenate([dx[0], dx[1]], axis=1)
    log_gamma = -jax.nn.softplus(decay)
    cum8 = jnp.dot(log_gamma, upper, precision=lax.Precision.HIGHEST, preferred_element_type=F32)
    beta8 = jax.nn.sigmoid(jnp.concatenate([bx[0], bx[1]], axis=1))
    pick = lambda rows: jnp.where(c == 0, rows[:OWN], rows[OWN:])
    cum, beta = pick(cum8), pick(beta8)
    last = cum[:, TOK - 1:]
    to_end = jnp.where(seg_row == seg_end, jnp.exp(last - cum), 0.0)
    through = jnp.where(seg_end == seg_prev, jnp.exp(last), 0.0)
    by_token = jnp.concatenate([cum, beta], axis=0).T
    in_first = seg_col == seg_prev

    xf[:HALO] = jnp.zeros((HALO, 1024), F32)
    for ref, lo, width in ((qx, 0, 256), (kx, 256, 256), (vx, 512, 512)):
        xf[HALO:, lo:lo + width] = ref[...].astype(F32)

    def activate(count):
        for w_ref, lo, width in ((cq_ref, 0, 256), (ck_ref, 256, 256), (cv_ref, 512, 512)):
            taps = w_ref[:, cols(c, width)]
            total = None
            for i in range(4):
                term = taps[i:i + 1] * xf[HALO - 3 + i:HALO - 3 + i + count, lo:lo + width]
                if i < 3:
                    term = term * keeps[3 - i][:count]
                total = term if total is None else total + term
            total = total * jax.nn.sigmoid(total)
            if lo < 512:
                for n in range(2):
                    head = total[:, n * DK:(n + 1) * DK]
                    norm = lax.rsqrt(jnp.sum(head * head, axis=-1, keepdims=True) + 1e-6)
                    act[:count, lo + n * DK:lo + (n + 1) * DK] = head * norm
            else:
                act[:count, lo:lo + width] = total

    activate(TOK)

    @pl.when(has_prev)
    def _():
        halo[0].wait_recv()

    xf[:HALO] = hx[...].astype(F32)
    activate(8)

    def lanes(size, height):
        where = lax.broadcasted_iota(jnp.int32, (height, 128), 1) // size
        return [(where == b).astype(BF16) for b in range(128 // size)]

    def expand(packed, size, masks, rows):
        zero = jnp.zeros((size, 128), BF16)
        out = []
        for b in range(TOK // size):
            src = rows(b)
            if src is None:
                out.append(jnp.concatenate([zero, zero], axis=1))
                continue
            half, inner = src * size // 128, src % (128 // size)
            piece = packed[:, halves[half]] * masks[inner]
            out.append(jnp.concatenate([piece, zero] if half == 0 else [zero, piece], axis=1))
        return jnp.concatenate(out, axis=0)

    def gather(low, size, masks, row_block, lane_block, count):
        both = []
        for half in range(2):
            total = None
            for p in range(count // 2):
                r, s = row_block(p), lane_block(p)
                piece = low[half, half][r * size:(r + 1) * size] * masks[s]
                total = piece if total is None else total + piece
            both.append(total)
        return jnp.concatenate(both, axis=1)

    every = range(OWN)
    kfs = [act[:, 256 + n * DK:256 + (n + 1) * DK] for n in range(2)]
    qfs = [act[:, n * DK:(n + 1) * DK] for n in range(2)]
    kbs = [kf.astype(BF16) for kf in kfs]
    k_ts = [kf.T for kf in kfs]
    k_tbs = [k_t.astype(BF16) for k_t in k_ts]
    grams = [dot(kbs[n], k_tbs[n]) for n in range(2)]
    cum_cols = [by_token[:, i:i + 1] for i in every]
    beta_cols = [by_token[:, OWN + i:OWN + i + 1] for i in every]
    start_cols = [jnp.where(in_first, jnp.exp(cum_cols[i]), 0.0) for i in every]

    pairs, lows = [], []
    for i in every:
        pair, low = {}, {}
        for r, s in quads:
            diff = cum_cols[i][halves[r]] - cum[i:i + 1, halves[s]]
            pair[r, s] = jnp.exp(jnp.where(same_doc[r, s], diff, -1e30))
            part = beta_cols[i][halves[r]] * grams[i // 2][halves[r], halves[s]] * pair[r, s]
            low[r, s] = (jnp.where(sub > lane, part, 0.0) if r == s else part).astype(BF16)
        pairs.append(pair)
        lows.append(low)

    m16 = lanes(16, 16)
    diag = lambda b: b
    eye16 = (lax.broadcasted_iota(jnp.int32, (16, TOK), 0) == lax.broadcasted_iota(jnp.int32, (16, TOK), 1) % 16).astype(F32)
    n1 = [-gather(lows[i], 16, m16, lambda p: p, lambda p: p, 16) for i in every]
    t = [eye16 + n1[i].astype(F32) for i in every]
    n2 = [dot(n1[i], expand(n1[i], 16, m16, diag)).astype(BF16) for i in every]
    power = n2
    for last_step in (False, False, True):
        wide = [expand(power[i], 16, m16, diag) for i in every]
        if last_step:
            t = [t[i] + dot(t[i].astype(BF16), wide[i]) for i in every]
        else:
            both = [dot(jnp.concatenate([power[i], t[i].astype(BF16)], axis=0), wide[i]) for i in every]
            power = [both[i][:16].astype(BF16) for i in every]
            t = [t[i] + both[i][16:] for i in every]

    for size in (16, 32, 64):
        masks = lanes(size, size)
        even = (lax.broadcasted_iota(jnp.int32, (size, TOK), 1) // size) % 2 == 0
        tb = [t[i].astype(BF16) for i in every]
        edge = [gather(lows[i], size, masks, lambda p: 2 * p + 1, lambda p: 2 * p, TOK // size // 2) for i in every]
        y = [dot(edge[i], expand(tb[i], size, masks, lambda b: b if b % 2 == 0 else None)).astype(BF16) for i in every]
        below = [dot(tb[i], expand(y[i], size, masks, lambda b: b - 1 if b % 2 else None)) for i in every]
        t = [jnp.concatenate([jnp.where(even, t[i], 0.0), jnp.where(even, -below[i], t[i])], axis=0) for i in every]

    rhs = []
    for i in every:
        v = act[:, 512 + i * DK:512 + (i + 1) * DK]
        rhs.append((beta_cols[i] * v, (beta_cols[i] * start_cols[i]) * kfs[i // 2]))
    tb = [t[i].astype(BF16) for i in every]
    rhs = [jnp.concatenate(rhs[i], axis=1) for i in every]
    uw_top = [dot(tb[i][:, :128], rhs[i][:128].astype(BF16)).astype(BF16) for i in every]
    rest = [(rhs[i][128:] - dot(lows[i][1, 0], uw_top[i])).astype(BF16) for i in every]
    uw = [jnp.concatenate([uw_top[i], dot(tb[i][:, 128:], rest[i]).astype(BF16)], axis=0) for i in every]
    kuw = [dot((k_ts[i // 2] * to_end[i:i + 1]).astype(BF16), uw[i]) for i in every]
    eye = (sub == lane).astype(F32)
    for i in every:
        mb[i, :, :DK] = (through[i:i + 1] * eye - kuw[i][:, DK:]).astype(BF16)
        mb[i, :, DK:] = kuw[i][:, :DK].astype(BF16)

    pl.semaphore_wait(told.at[3], 1)
    pl.semaphore_wait(told.at[4], 1)
    sends = []
    for i in every:
        owner = OWN * c + i
        sends.append((owner, pltpu.make_async_remote_copy(
            mb.at[i], rbuf.at[z], as_.at[i], ar.at[z], device_id={"ctx": at(owner)}, device_id_type=MESH,
        )))
    for owner, send in sends:
        @pl.when(z != owner)
        def _():
            send.start()

    @pl.when(own)
    def _():
        rbuf[z] = mb[head_at]

    scores = [dot(qfs[n].astype(BF16), k_tbs[n]) for n in range(2)]
    for i in every:
        inside = {q: (scores[i // 2][halves[q[0]], halves[q[1]]] * pairs[i][q]).astype(BF16) for q in quads}
        top = dot(inside[0, 0], uw_top[i])
        bottom = dot(jnp.concatenate([inside[1, 0], inside[1, 1]], axis=1), uw[i])
        q_start = qfs[i // 2] * start_cols[i]
        oloc[i, :128] = top[:, :DK]
        oloc[i, 128:] = bottom[:, :DK]
        qeff[i, :128] = (q_start[:128] - top[:, DK:]).astype(BF16)
        qeff[i, 128:] = (q_start[128:] - bottom[:, DK:]).astype(BF16)
    trade[5].wait_recv()
    gate = gx[...].astype(F32)
    gated[...] = gate * jax.nn.sigmoid(gate) * jnp.concatenate([gain_ref[...]] * OWN, axis=1)

    mine_at = jnp.where(own, head_at, 0)
    back = []
    for k in range(1, CHIPS):
        back.append(pltpu.make_async_remote_copy(
            sout.at[k], sbuf.at[mine_at], ss.at[k], sr.at[mine_at], device_id={"ctx": ring(k)}, device_id_type=MESH,
        ))
    ahead = pltpu.make_async_remote_copy(q8, s0buf, ys, yr, device_id={"ctx": up}, device_id_type=MESH)

    @pl.when(own)
    def _():
        for k in range(1, CHIPS):
            j = lax.rem(z + k, CHIPS)
            pltpu.make_async_remote_copy(
                mb.at[0], rbuf.at[j], as_.at[0], ar.at[j], device_id={"ctx": ring(k)}, device_id_type=MESH,
            ).wait_recv()

        def then(later, earlier):
            joined = dot(later[:, :DK], earlier)
            return jnp.concatenate([joined[:, :DK], joined[:, DK:] + later[:, DK:].astype(F32)], axis=1).astype(BF16)

        one = [rbuf[j] for j in range(CHIPS)]
        two = [then(one[2 * j + 1], one[2 * j]) for j in range(4)]
        four = [then(two[1], two[0]), then(two[3], two[2])]
        q8[...] = (dot(four[1][:, :DK], four[0][:, DK:]) + four[1][:, DK:].astype(F32)).astype(BF16)

        @pl.when(has_up)
        def _():
            ahead.start()

        six = then(two[2], four[0])
        start = jnp.concatenate([eye, jnp.zeros((DK, DK), F32)], axis=1).astype(BF16)
        for j, value in enumerate((
            start, one[0], two[0], then(one[2], two[0]), four[0], then(one[4], four[0]), six, then(one[6], six),
        )):
            pre[j] = value

        @pl.when(has_down)
        def _():
            ahead.wait_recv()

        s0 = s0buf[...]
        for k in (4, 3, 5, 2, 6, 1, 7, 0):
            step = pre[lax.rem(z + k, CHIPS)]
            state = (dot(step[:, :DK], s0) + step[:, DK:].astype(F32)).astype(BF16)
            if k:
                sout[k] = state
                back[k - 1].start()
            else:
                sbuf[head_at] = state

    for i in every:
        @pl.when(z != OWN * c + i)
        def _():
            pltpu.make_async_remote_copy(
                sout.at[0], sbuf.at[i], ss.at[0], sr.at[i], device_id={"ctx": partner}, device_id_type=MESH,
            ).wait_recv()
    theirs = pl.ds(pl.multiple_of(ROWS * (1 - c), 16), ROWS)
    swap = pltpu.make_async_remote_copy(
        mx.at[theirs], mixfull, ms, mr, device_id={"ctx": partner}, device_id_type=MESH,
    )
    for tokens in (theirs, mine):
        for i in every:
            o = oloc[i, tokens] + dot(qeff[i, tokens], sbuf[i])
            normed = o * lax.rsqrt(jnp.mean(o * o, axis=-1, keepdims=True) + 1e-6)
            mx[tokens, i * DK:(i + 1) * DK] = (normed * gated[tokens, i * DK:(i + 1) * DK]).astype(BF16)
        if tokens is theirs:
            swap.start()
    w_copy.wait()

    half = OWN * DK
    rows = lambda core: pl.ds(pl.multiple_of(core * half, 128), half)
    width = w_vm.shape[1] // 4
    mixed = mx[mine]
    order = (2, 1, 3, 0)
    for k in order:
        own_part[k] = dot(mixed, w_vm[rows(c), cols(lax.rem(x + k, n_x), width)])
    pl.semaphore_wait(told.at[2], 1)
    swap.wait_recv()
    mixed = mixfull[...]
    parts = []
    for k in order:
        to = lax.rem(x + k, n_x)
        part = (own_part[k] + dot(mixed, w_vm[rows(1 - c), cols(to, width)])).astype(BF16)
        if k == 0:
            total = part.astype(F32)
            continue
        sendp[k - 1] = part
        parts.append(pltpu.make_async_remote_copy(
            sendp.at[k - 1], recvp.at[k - 1], ps.at[k - 1], pr.at[k - 1], device_id={"head": to}, device_id_type=MESH,
        ))
        parts[-1].start()
    for part, k in zip(parts, order):
        part.wait_recv()
        total = total + recvp[k - 1].astype(F32)
    out_ref[...] = total.T.astype(BF16)

    for copy in trade + [swap] + parts:
        copy.wait_send()

    @pl.when(sends_halo)
    def _():
        for copy in halo:
            copy.wait_send()

    for owner, send in sends:
        @pl.when(z != owner)
        def _():
            send.wait_send()

    @pl.when(own & has_up)
    def _():
        ahead.wait_send()

    @pl.when(own)
    def _():
        for copy in back:
            copy.wait_send()


def body(
    query_in, key_in, value_in, gate_in, conv_query, conv_key, conv_value,
    decay_in, beta_in, norm_gain, doc_lengths, out_weight,
):
    anywhere, vmem = pl.BlockSpec(memory_space=pl.ANY), pl.BlockSpec(memory_space=pltpu.VMEM)
    dma = pltpu.SemaphoreType.DMA
    features = out_weight.shape[1] // 4
    return pl.pallas_call(
        kernel,
        out_shape=jax.ShapeDtypeStruct((features, ROWS), BF16),
        in_specs=[anywhere] * 7 + [vmem] * 5,
        out_specs=vmem,
        scratch_shapes=[
            pltpu.VMEM((TOK, 256), BF16),
            pltpu.VMEM((TOK, 256), BF16),
            pltpu.VMEM((TOK, 512), BF16),
            pltpu.VMEM((TOK, 512), BF16),
            pltpu.VMEM((2, 8, ROWS), F32),
            pltpu.VMEM((2, 8, ROWS), F32),
            pltpu.VMEM((2, HALO, 1024), BF16),
            pltpu.VMEM((HALO, 1024), BF16),
            pltpu.VMEM((HALO + TOK, 1024), F32),
            pltpu.VMEM((TOK, 1024), F32),
            pltpu.VMEM(out_weight.shape, BF16),
            pltpu.VMEM((OWN, DK, 2 * DK), BF16),
            pltpu.VMEM((OWN, TOK, DK), BF16),
            pltpu.VMEM((OWN, TOK, DK), F32),
            pltpu.VMEM((CHIPS, DK, 2 * DK), BF16),
            pltpu.VMEM((CHIPS, DK, 2 * DK), BF16),
            pltpu.VMEM((DK, DK), BF16),
            pltpu.VMEM((DK, DK), BF16),
            pltpu.VMEM((CHIPS, DK, DK), BF16),
            pltpu.VMEM((OWN, DK, DK), BF16),
            pltpu.VMEM((TOK, OWN * DK), F32),
            pltpu.VMEM((TOK, OWN * DK), BF16),
            pltpu.VMEM((ROWS, OWN * DK), BF16),
            pltpu.VMEM((4, ROWS, features), F32),
            pltpu.VMEM((3, ROWS, features), BF16),
            pltpu.VMEM((3, ROWS, features), BF16),
            dma((7,)), dma((6,)), dma((6,)), dma((2, 3)), dma((2,)), dma,
            dma((OWN,)), dma((CHIPS,)), dma, dma, dma((CHIPS,)), dma((OWN,)),
            dma, dma, dma((3,)), dma((3,)), pltpu.SemaphoreType.REGULAR((5,)),
        ],
        compiler_params=pltpu.CompilerParams(
            collective_id=0, has_side_effects=True, vmem_limit_bytes=56 << 20
        ),
        name="mixer",
    )(
        query_in, key_in, value_in, gate_in, decay_in, beta_in, out_weight,
        conv_query, conv_key, conv_value, doc_lengths.reshape(1, -1), norm_gain.reshape(1, -1),
    )


def solution(mesh):
    return jax.shard_map(
        body,
        mesh=mesh,
        in_specs=(
            P("ctx", "head"), P("ctx", "head"), P("ctx", "head"), P("ctx", "head"),
            P(None, "head"), P(None, "head"), P(None, "head"),
            P("head", "ctx"), P("head", "ctx"), P(), P(), P("head", None),
        ),
        out_specs=P("head", "ctx"),
        check_vma=False,
    )
```

```python
import jax
import jax.numpy as jnp
from jax import lax
from jax.experimental import pallas as pl
from jax.experimental.pallas import tpu as pltpu
from jax.sharding import PartitionSpec as P

MESH = pl.DeviceIdType.MESH
F32, BF16 = jnp.float32, jnp.bfloat16
DK = 128
ROWS = 128
TOK = 256
HALO = 16
CHIPS = 8
OWN = 4


def dot(a, b):
    return jnp.dot(a, b, preferred_element_type=F32)


def fine_dot(a, b):
    high = a.astype(BF16)
    return dot(high, b) + dot((a - high.astype(F32)).astype(BF16), b)


def kernel(
    q_hbm, k_hbm, v_hbm, g_hbm, dec_hbm, beta_hbm, w_hbm,
    cq_ref, ck_ref, cv_ref, docs_ref, gain_ref,
    out_ref,
    qx, kx, vx, gx, dx, bx, hb, hx, xf, act, w_vm,
    mb, qeff, oloc, rbuf, pre, q8, s0buf, sout, sbuf, gated, mx, mixfull, own_part, sendp, via, joined, recvp,
    lsem, xs, xr, hl, hs, hr, as_, ar, ys, yr, ss, sr, ms, mr, ps, pr, told,
):
    ctx, x = lax.axis_index("ctx"), lax.axis_index("head")
    n_ctx, n_x = lax.axis_size("ctx"), lax.axis_size("head")
    c = lax.rem(ctx, 2)
    chip = ctx // 2
    z = lax.rem(chip, CHIPS)
    line = ctx - 2 * z - c
    n_chips = n_ctx // 2
    partner = chip * 2 + 1 - c
    prev_tail = jnp.maximum(chip - 1, 0) * 2 + 1
    next_head = jnp.minimum(chip + 1, n_chips - 1) * 2
    has_prev, has_next = chip > 0, chip < n_chips - 1
    sends_halo = (c == 1) & has_next
    own = z // OWN == c
    head_at = z - OWN * c
    has_up, has_down = ctx < n_ctx - 2 * CHIPS, ctx >= 2 * CHIPS
    up = jnp.minimum(ctx + 2 * CHIPS, n_ctx - 1)
    down = jnp.maximum(ctx - 2 * CHIPS, 0)

    def at(chip_z):
        return line + 2 * chip_z + c

    w_copy = pltpu.make_async_copy(w_hbm, w_vm, lsem.at[0])
    w_copy.start()
    cols = lambda core, width: pl.ds(pl.multiple_of(core * width, 128), width)
    mine = pl.ds(pl.multiple_of(ROWS * c, 16), ROWS)
    local = []
    for n, (src, dst) in enumerate((
        (q_hbm.at[:, cols(c, 256)], qx.at[mine]),
        (k_hbm.at[:, cols(c, 256)], kx.at[mine]),
        (v_hbm.at[:, cols(c, 512)], vx.at[mine]),
        (g_hbm.at[:, cols(c, 512)], gx.at[mine]),
        (dec_hbm, dx.at[c]),
        (beta_hbm, bx.at[c]),
    )):
        local.append(pltpu.make_async_copy(src, dst, lsem.at[n + 1]))
        local[-1].start()

    pack = []
    for core in range(2):
        for n, (src, lo, width) in enumerate(((q_hbm, 0, 256), (k_hbm, 256, 256), (v_hbm, 512, 512))):
            pack.append(pltpu.make_async_copy(
                src.at[pl.ds(ROWS - HALO, HALO), pl.ds(core * width, width)],
                hb.at[core, :, pl.ds(lo, width)], hl.at[core, n],
            ))

    @pl.when(sends_halo)
    def _():
        for copy in pack:
            copy.start()

    @pl.when(chip == 0)
    def _():
        hx[...] = jnp.zeros_like(hx)

    @pl.when(~has_down)
    def _():
        s0buf[...] = jnp.zeros_like(s0buf)

    barrier = pltpu.get_barrier_semaphore()

    def signal(sem, **device):
        pl.semaphore_signal(sem, inc=1, device_id=device, device_id_type=MESH)

    def ring(k):
        return at(lax.rem(z + k + CHIPS, CHIPS))

    x_next, x_prev = lax.rem(x + 1, n_x), lax.rem(x + n_x - 1, n_x)
    signal(barrier, ctx=partner)
    signal(barrier, head=x_next)
    signal(barrier, head=x_prev)
    signal(barrier, ctx=ring(1))
    signal(barrier, ctx=ring(-1))

    @pl.when(has_prev)
    def _():
        signal(barrier, ctx=prev_tail)

    @pl.when(has_down)
    def _():
        signal(barrier, ctx=down)

    pl.semaphore_wait(barrier, 5 + jnp.where(sends_halo, 2, 0) + jnp.where(has_up, 1, 0))

    halo = []
    for core in range(2):
        halo.append(pltpu.make_async_remote_copy(
            hb.at[core], hx, hs.at[core], hr, device_id={"ctx": next_head + core}, device_id_type=MESH,
        ))

    @pl.when(sends_halo)
    def _():
        for copy in pack:
            copy.wait()
        for copy in halo:
            copy.start()

    trade = []
    for n, (src, dst) in enumerate((
        (dec_hbm, dx.at[c]),
        (beta_hbm, bx.at[c]),
        (k_hbm.at[:, cols(1 - c, 256)], kx.at[mine]),
        (q_hbm.at[:, cols(1 - c, 256)], qx.at[mine]),
        (v_hbm.at[:, cols(1 - c, 512)], vx.at[mine]),
        (g_hbm.at[:, cols(1 - c, 512)], gx.at[mine]),
    )):
        trade.append(pltpu.make_async_remote_copy(
            src, dst, xs.at[n], xr.at[n], device_id={"ctx": partner}, device_id_type=MESH,
        ))
        trade[-1].start()

    signal(told.at[0], ctx=ring(1))
    signal(told.at[1], ctx=ring(-1))

    first = chip * TOK
    sub = lax.broadcasted_iota(jnp.int32, (128, 128), 0)
    lane = lax.broadcasted_iota(jnp.int32, (128, 128), 1)
    lens = jnp.broadcast_to(docs_ref[...].astype(F32), (128, 128))
    starts_col = jnp.sum(jnp.where(lane < sub, lens, 0.0), axis=1, keepdims=True)
    starts_row = jnp.sum(jnp.where(sub < lane, lens.T, 0.0), axis=0, keepdims=True)
    pos_row = (first + lax.broadcasted_iota(jnp.int32, (128, TOK), 1)).astype(F32)
    seg_row = jnp.sum(jnp.where(starts_col <= pos_row, 1.0, 0.0), axis=0, keepdims=True)
    seg_prev = jnp.sum(jnp.where(starts_col <= (first - 1).astype(F32), 1.0, 0.0), axis=0, keepdims=True)
    seg_end = jnp.sum(jnp.where(starts_col <= (first + TOK - 1).astype(F32), 1.0, 0.0), axis=0, keepdims=True)
    pos_col = first + lax.broadcasted_iota(jnp.int32, (TOK, 128), 0)

    def seg_at(back):
        return jnp.sum(jnp.where(starts_row <= (pos_col - back).astype(F32), 1.0, 0.0), axis=1, keepdims=True)

    seg_col = seg_at(0)
    keeps = [None] + [(seg_at(j) == seg_col).astype(F32) for j in range(1, 4)]
    upper = (lax.broadcasted_iota(jnp.int32, (TOK, TOK), 0) <= lax.broadcasted_iota(jnp.int32, (TOK, TOK), 1)).astype(F32)
    halves = (slice(0, 128), slice(128, 256))
    quads = ((0, 0), (1, 0), (1, 1))
    same_doc = {}
    for r, s in quads:
        same = seg_col[halves[r]] == seg_row[:, halves[s]]
        same_doc[r, s] = same & (sub >= lane) if r == s else same

    for copy in local[4:]:
        copy.wait()
    for copy in trade[:2]:
        copy.wait_recv()

    decay = jnp.concatenate([dx[0], dx[1]], axis=1)
    log_gamma = -jax.nn.softplus(decay)
    cum8 = jnp.dot(log_gamma, upper, precision=lax.Precision.HIGHEST, preferred_element_type=F32)
    beta8 = jax.nn.sigmoid(jnp.concatenate([bx[0], bx[1]], axis=1))
    pick = lambda rows: jnp.where(c == 0, rows[:OWN], rows[OWN:])
    cum, beta = pick(cum8), pick(beta8)
    last = cum[:, TOK - 1:]
    to_end = jnp.where(seg_row == seg_end, jnp.exp(last - cum), 0.0)
    through = jnp.where(seg_end == seg_prev, jnp.exp(last), 0.0)
    by_token = jnp.concatenate([cum, beta], axis=0).T
    in_first = seg_col == seg_prev

    pl.semaphore_wait(told.at[0], 1)
    pl.semaphore_wait(told.at[1], 1)
    signal(told.at[2], ctx=ring(2))
    signal(told.at[3], ctx=ring(-2))

    for copy in local[:4]:
        copy.wait()
    for copy in trade[2:5]:
        copy.wait_recv()

    xf[:HALO] = jnp.zeros((HALO, 1024), F32)
    for ref, lo, width in ((qx, 0, 256), (kx, 256, 256), (vx, 512, 512)):
        xf[HALO:, lo:lo + width] = ref[...].astype(F32)

    def activate(count):
        for w_ref, lo, width in ((cq_ref, 0, 256), (ck_ref, 256, 256), (cv_ref, 512, 512)):
            taps = w_ref[:, cols(c, width)]
            total = None
            for i in range(4):
                term = taps[i:i + 1] * xf[HALO - 3 + i:HALO - 3 + i + count, lo:lo + width]
                if i < 3:
                    term = term * keeps[3 - i][:count]
                total = term if total is None else total + term
            total = total * jax.nn.sigmoid(total)
            if lo < 512:
                for n in range(2):
                    head = total[:, n * DK:(n + 1) * DK]
                    norm = lax.rsqrt(jnp.sum(head * head, axis=-1, keepdims=True) + 1e-6)
                    act[:count, lo + n * DK:lo + (n + 1) * DK] = head * norm
            else:
                act[:count, lo:lo + width] = total

    activate(TOK)

    @pl.when(has_prev)
    def _():
        halo[0].wait_recv()

    xf[:HALO] = hx[...].astype(F32)
    activate(8)

    def lanes(size, height):
        where = lax.broadcasted_iota(jnp.int32, (height, 128), 1) // size
        return [(where == b).astype(BF16) for b in range(128 // size)]

    def expand(packed, size, masks, rows):
        zero = jnp.zeros((size, 128), BF16)
        out = []
        for b in range(TOK // size):
            src = rows(b)
            if src is None:
                out.append(jnp.concatenate([zero, zero], axis=1))
                continue
            half, inner = src * size // 128, src % (128 // size)
            piece = packed[:, halves[half]] * masks[inner]
            out.append(jnp.concatenate([piece, zero] if half == 0 else [zero, piece], axis=1))
        return jnp.concatenate(out, axis=0)

    def gather(low, size, masks, row_block, lane_block, count):
        both = []
        for half in range(2):
            total = None
            for p in range(count // 2):
                r, s = row_block(p), lane_block(p)
                piece = low[half, half][r * size:(r + 1) * size] * masks[s]
                total = piece if total is None else total + piece
            both.append(total)
        return jnp.concatenate(both, axis=1)

    every = range(OWN)
    kfs = [act[:, 256 + n * DK:256 + (n + 1) * DK] for n in range(2)]
    qfs = [act[:, n * DK:(n + 1) * DK] for n in range(2)]
    kbs = [kf.astype(BF16) for kf in kfs]
    k_ts = [kf.T for kf in kfs]
    k_tbs = [k_t.astype(BF16) for k_t in k_ts]
    grams = [dot(kbs[n], k_tbs[n]) for n in range(2)]
    cum_cols = [by_token[:, i:i + 1] for i in every]
    beta_cols = [by_token[:, OWN + i:OWN + i + 1] for i in every]
    start_cols = [jnp.where(in_first, jnp.exp(cum_cols[i]), 0.0) for i in every]

    pairs, lows = [], []
    for i in every:
        pair, low = {}, {}
        for r, s in quads:
            diff = cum_cols[i][halves[r]] - cum[i:i + 1, halves[s]]
            pair[r, s] = jnp.exp(jnp.where(same_doc[r, s], diff, -1e30))
            part = beta_cols[i][halves[r]] * grams[i // 2][halves[r], halves[s]] * pair[r, s]
            low[r, s] = (jnp.where(sub > lane, part, 0.0) if r == s else part).astype(BF16)
        pairs.append(pair)
        lows.append(low)

    m16 = lanes(16, 16)
    diag = lambda b: b
    eye16 = (lax.broadcasted_iota(jnp.int32, (16, TOK), 0) == lax.broadcasted_iota(jnp.int32, (16, TOK), 1) % 16).astype(F32)
    n1 = [-gather(lows[i], 16, m16, lambda p: p, lambda p: p, 16) for i in every]
    t = [eye16 + n1[i].astype(F32) for i in every]
    n2 = [dot(n1[i], expand(n1[i], 16, m16, diag)).astype(BF16) for i in every]
    power = n2
    for last_step in (False, False, True):
        wide = [expand(power[i], 16, m16, diag) for i in every]
        if last_step:
            t = [t[i] + dot(t[i].astype(BF16), wide[i]) for i in every]
        else:
            both = [dot(jnp.concatenate([power[i], t[i].astype(BF16)], axis=0), wide[i]) for i in every]
            power = [both[i][:16].astype(BF16) for i in every]
            t = [t[i] + both[i][16:] for i in every]

    for size in (16, 32, 64):
        masks = lanes(size, size)
        even = (lax.broadcasted_iota(jnp.int32, (size, TOK), 1) // size) % 2 == 0
        tb = [t[i].astype(BF16) for i in every]
        edge = [gather(lows[i], size, masks, lambda p: 2 * p + 1, lambda p: 2 * p, TOK // size // 2) for i in every]
        y = [dot(edge[i], expand(tb[i], size, masks, lambda b: b if b % 2 == 0 else None)).astype(BF16) for i in every]
        below = [dot(tb[i], expand(y[i], size, masks, lambda b: b - 1 if b % 2 else None)) for i in every]
        t = [jnp.concatenate([jnp.where(even, t[i], 0.0), jnp.where(even, -below[i], t[i])], axis=0) for i in every]

    rhs = []
    for i in every:
        v = act[:, 512 + i * DK:512 + (i + 1) * DK]
        rhs.append((beta_cols[i] * v, (beta_cols[i] * start_cols[i]) * kfs[i // 2]))
    tb = [t[i].astype(BF16) for i in every]
    rhs = [jnp.concatenate(rhs[i], axis=1) for i in every]
    uw_top = [dot(tb[i][:, :128], rhs[i][:128].astype(BF16)).astype(BF16) for i in every]
    rest = [(rhs[i][128:] - dot(lows[i][1, 0], uw_top[i])).astype(BF16) for i in every]
    uw = [jnp.concatenate([uw_top[i], dot(tb[i][:, 128:], rest[i]).astype(BF16)], axis=0) for i in every]
    kuw = [fine_dot(k_ts[i // 2] * to_end[i:i + 1], uw[i]) for i in every]
    eye = (sub == lane).astype(F32)
    for i in every:
        mb[i, :, :DK] = (through[i:i + 1] * eye - kuw[i][:, DK:]).astype(BF16)
        mb[i, :, DK:] = kuw[i][:, :DK].astype(BF16)

    pl.semaphore_wait(told.at[2], 1)
    pl.semaphore_wait(told.at[3], 1)
    sends = []
    for i in every:
        owner = OWN * c + i
        sends.append((owner, pltpu.make_async_remote_copy(
            mb.at[i], rbuf.at[z], as_.at[i], ar.at[z], device_id={"ctx": at(owner)}, device_id_type=MESH,
        )))
    for owner, send in sends:
        @pl.when(z != owner)
        def _():
            send.start()

    @pl.when(own)
    def _():
        rbuf[z] = mb[head_at]

    scores = [dot(qfs[n].astype(BF16), k_tbs[n]) for n in range(2)]
    for i in every:
        inside = {q: scores[i // 2][halves[q[0]], halves[q[1]]] * pairs[i][q] for q in quads}
        top = fine_dot(inside[0, 0], uw_top[i])
        bottom = fine_dot(jnp.concatenate([inside[1, 0], inside[1, 1]], axis=1), uw[i])
        q_start = qfs[i // 2] * start_cols[i]
        oloc[i, :128] = top[:, :DK]
        oloc[i, 128:] = bottom[:, :DK]
        qeff[i, :128] = (q_start[:128] - top[:, DK:]).astype(BF16)
        qeff[i, 128:] = (q_start[128:] - bottom[:, DK:]).astype(BF16)
    trade[5].wait_recv()
    gate = gx[...].astype(F32)
    gated[...] = gate * jax.nn.sigmoid(gate) * jnp.concatenate([gain_ref[...]] * OWN, axis=1)

    mine_at = jnp.where(own, head_at, 0)
    back = []
    for k in range(1, CHIPS):
        back.append(pltpu.make_async_remote_copy(
            sout.at[k], sbuf.at[mine_at], ss.at[k], sr.at[mine_at], device_id={"ctx": ring(k)}, device_id_type=MESH,
        ))
    ahead = pltpu.make_async_remote_copy(q8, s0buf, ys, yr, device_id={"ctx": up}, device_id_type=MESH)

    @pl.when(own)
    def _():
        for k in range(1, CHIPS):
            j = lax.rem(z + k, CHIPS)
            pltpu.make_async_remote_copy(
                mb.at[0], rbuf.at[j], as_.at[0], ar.at[j], device_id={"ctx": ring(k)}, device_id_type=MESH,
            ).wait_recv()

        def then(later, earlier):
            joined = dot(later[:, :DK], earlier)
            return jnp.concatenate([joined[:, :DK], joined[:, DK:] + later[:, DK:].astype(F32)], axis=1).astype(BF16)

        one = [rbuf[j] for j in range(CHIPS)]
        two = [then(one[2 * j + 1], one[2 * j]) for j in range(4)]
        four = [then(two[1], two[0]), then(two[3], two[2])]
        q8[...] = (dot(four[1][:, :DK], four[0][:, DK:]) + four[1][:, DK:].astype(F32)).astype(BF16)

        @pl.when(has_up)
        def _():
            ahead.start()

        six = then(two[2], four[0])
        start = jnp.concatenate([eye, jnp.zeros((DK, DK), F32)], axis=1).astype(BF16)
        for j, value in enumerate((
            start, one[0], two[0], then(one[2], two[0]), four[0], then(one[4], four[0]), six, then(one[6], six),
        )):
            pre[j] = value

        @pl.when(has_down)
        def _():
            ahead.wait_recv()

        s0 = s0buf[...]
        for k in (4, 3, 5, 2, 6, 1, 7, 0):
            step = pre[lax.rem(z + k, CHIPS)]
            state = (dot(step[:, :DK], s0) + step[:, DK:].astype(F32)).astype(BF16)
            if k:
                sout[k] = state
                back[k - 1].start()
            else:
                sbuf[head_at] = state

    for i in every:
        @pl.when(z != OWN * c + i)
        def _():
            pltpu.make_async_remote_copy(
                sout.at[0], sbuf.at[i], ss.at[0], sr.at[i], device_id={"ctx": partner}, device_id_type=MESH,
            ).wait_recv()
    theirs = pl.ds(pl.multiple_of(ROWS * (1 - c), 16), ROWS)
    swap = pltpu.make_async_remote_copy(
        mx.at[theirs], mixfull, ms, mr, device_id={"ctx": partner}, device_id_type=MESH,
    )
    for tokens in (theirs, mine):
        for i in every:
            o = oloc[i, tokens] + dot(qeff[i, tokens], sbuf[i])
            normed = o * lax.rsqrt(jnp.mean(o * o, axis=-1, keepdims=True) + 1e-6)
            mx[tokens, i * DK:(i + 1) * DK] = (normed * gated[tokens, i * DK:(i + 1) * DK]).astype(BF16)
        if tokens is theirs:
            swap.start()
    w_copy.wait()

    half = OWN * DK
    rows = lambda core: pl.ds(pl.multiple_of(core * half, 128), half)
    width = w_vm.shape[1] // 4
    mixed = mx[mine]
    order = (2, 1, 3, 0)
    for k in order:
        own_part[k] = dot(mixed, w_vm[rows(c), cols(lax.rem(x + k, n_x), width)])
    swap.wait_recv()
    mixed = mixfull[...]

    def part(k):
        block = cols(lax.rem(x + k, n_x), width)
        return (own_part[k] + dot(mixed, w_vm[rows(1 - c), block])).astype(BF16)

    sent = []

    def pass_on(n, src, dst, to):
        sent.append(pltpu.make_async_remote_copy(
            src, dst, ps.at[n], pr.at[n], device_id={"head": to}, device_id_type=MESH,
        ))
        sent[-1].start()

    early, late = pl.ds(0, ROWS // 2), pl.ds(ROWS // 2, ROWS // 2)
    sendp[1] = part(2)
    pass_on(0, sendp.at[1, early], via.at[0], x_next)
    pass_on(1, sendp.at[1, late], via.at[1], x_prev)
    sendp[0] = part(1)
    pass_on(2, sendp.at[0, late], recvp.at[0, late], x_next)
    sendp[2] = part(3)
    pass_on(3, sendp.at[2, early], recvp.at[1, early], x_prev)
    total = part(0).astype(F32)
    sent[0].wait_recv()
    joined[0] = (sendp[0, early].astype(F32) + via[0].astype(F32)).astype(BF16)
    pass_on(4, joined.at[0], recvp.at[0, early], x_next)
    sent[1].wait_recv()
    joined[1] = (sendp[2, late].astype(F32) + via[1].astype(F32)).astype(BF16)
    pass_on(5, joined.at[1], recvp.at[1, late], x_prev)
    for copy in sent[2:]:
        copy.wait_recv()
    out_ref[...] = (total + recvp[0].astype(F32) + recvp[1].astype(F32)).T.astype(BF16)

    for copy in trade + [swap] + sent:
        copy.wait_send()

    @pl.when(sends_halo)
    def _():
        for copy in halo:
            copy.wait_send()

    for owner, send in sends:
        @pl.when(z != owner)
        def _():
            send.wait_send()

    @pl.when(own & has_up)
    def _():
        ahead.wait_send()

    @pl.when(own)
    def _():
        for copy in back:
            copy.wait_send()


def body(
    query_in, key_in, value_in, gate_in, conv_query, conv_key, conv_value,
    decay_in, beta_in, norm_gain, doc_lengths, out_weight,
):
    anywhere, vmem = pl.BlockSpec(memory_space=pl.ANY), pl.BlockSpec(memory_space=pltpu.VMEM)
    dma = pltpu.SemaphoreType.DMA
    features = out_weight.shape[1] // 4
    return pl.pallas_call(
        kernel,
        out_shape=jax.ShapeDtypeStruct((features, ROWS), BF16),
        in_specs=[anywhere] * 7 + [vmem] * 5,
        out_specs=vmem,
        scratch_shapes=[
            pltpu.VMEM((TOK, 256), BF16),
            pltpu.VMEM((TOK, 256), BF16),
            pltpu.VMEM((TOK, 512), BF16),
            pltpu.VMEM((TOK, 512), BF16),
            pltpu.VMEM((2, 8, ROWS), F32),
            pltpu.VMEM((2, 8, ROWS), F32),
            pltpu.VMEM((2, HALO, 1024), BF16),
            pltpu.VMEM((HALO, 1024), BF16),
            pltpu.VMEM((HALO + TOK, 1024), F32),
            pltpu.VMEM((TOK, 1024), F32),
            pltpu.VMEM(out_weight.shape, BF16),
            pltpu.VMEM((OWN, DK, 2 * DK), BF16),
            pltpu.VMEM((OWN, TOK, DK), BF16),
            pltpu.VMEM((OWN, TOK, DK), F32),
            pltpu.VMEM((CHIPS, DK, 2 * DK), BF16),
            pltpu.VMEM((CHIPS, DK, 2 * DK), BF16),
            pltpu.VMEM((DK, DK), BF16),
            pltpu.VMEM((DK, DK), BF16),
            pltpu.VMEM((CHIPS, DK, DK), BF16),
            pltpu.VMEM((OWN, DK, DK), BF16),
            pltpu.VMEM((TOK, OWN * DK), F32),
            pltpu.VMEM((TOK, OWN * DK), BF16),
            pltpu.VMEM((ROWS, OWN * DK), BF16),
            pltpu.VMEM((4, ROWS, features), F32),
            pltpu.VMEM((3, ROWS, features), BF16),
            pltpu.VMEM((2, ROWS // 2, features), BF16),
            pltpu.VMEM((2, ROWS // 2, features), BF16),
            pltpu.VMEM((2, ROWS, features), BF16),
            dma((7,)), dma((6,)), dma((6,)), dma((2, 3)), dma((2,)), dma,
            dma((OWN,)), dma((CHIPS,)), dma, dma, dma((CHIPS,)), dma((OWN,)),
            dma, dma, dma((6,)), dma((6,)), pltpu.SemaphoreType.REGULAR((4,)),
        ],
        compiler_params=pltpu.CompilerParams(
            collective_id=0, has_side_effects=True, vmem_limit_bytes=56 << 20
        ),
        name="mixer",
    )(
        query_in, key_in, value_in, gate_in, decay_in, beta_in, out_weight,
        conv_query, conv_key, conv_value, doc_lengths.reshape(1, -1), norm_gain.reshape(1, -1),
    )


def solution(mesh):
    return jax.shard_map(
        body,
        mesh=mesh,
        in_specs=(
            P("ctx", "head"), P("ctx", "head"), P("ctx", "head"), P("ctx", "head"),
            P(None, "head"), P(None, "head"), P(None, "head"),
            P("head", "ctx"), P("head", "ctx"), P(), P(), P("head", None),
        ),
        out_specs=P("head", "ctx"),
        check_vma=False,
    )
```

```python
import jax
import jax.numpy as jnp
from jax import lax
from jax.experimental import pallas as pl
from jax.experimental.pallas import tpu as pltpu
from jax.sharding import PartitionSpec as P

MESH = pl.DeviceIdType.MESH
F32, BF16 = jnp.float32, jnp.bfloat16
DK = 128
ROWS = 128
TOK = 256
HALO = 16
CHIPS = 8
OWN = 4


def dot(a, b):
    return jnp.dot(a, b, preferred_element_type=F32)


def fine_dot(a, b):
    high = a.astype(BF16)
    return dot(high, b) + dot((a - high.astype(F32)).astype(BF16), b)


def kernel(
    q_hbm, k_hbm, v_hbm, g_hbm, dec_hbm, beta_hbm, w_hbm,
    cq_ref, ck_ref, cv_ref, docs_ref, gain_ref,
    out_ref,
    qx, kx, vx, gx, dx, bx, hb, hx, xf, act, w_vm,
    mb, qeff, oloc, rbuf, pre, q8, s0buf, sout, sbuf, gated, mx, mixfull, own_part, sendp, via, joined, recvp,
    lsem, xs, xr, hl, hs, hr, as_, ar, ys, yr, ss, sr, ms, mr, ps, pr, told,
):
    ctx, x = lax.axis_index("ctx"), lax.axis_index("head")
    n_ctx, n_x = lax.axis_size("ctx"), lax.axis_size("head")
    c = lax.rem(ctx, 2)
    chip = ctx // 2
    z = lax.rem(chip, CHIPS)
    line = ctx - 2 * z - c
    n_chips = n_ctx // 2
    partner = chip * 2 + 1 - c
    prev_tail = jnp.maximum(chip - 1, 0) * 2 + 1
    next_head = jnp.minimum(chip + 1, n_chips - 1) * 2
    has_prev, has_next = chip > 0, chip < n_chips - 1
    sends_halo = (c == 1) & has_next
    own = z // OWN == c
    head_at = z - OWN * c
    has_up, has_down = ctx < n_ctx - 2 * CHIPS, ctx >= 2 * CHIPS
    up = jnp.minimum(ctx + 2 * CHIPS, n_ctx - 1)
    down = jnp.maximum(ctx - 2 * CHIPS, 0)

    def at(chip_z):
        return line + 2 * chip_z + c

    w_copy = pltpu.make_async_copy(w_hbm, w_vm, lsem.at[0])
    w_copy.start()
    cols = lambda core, width: pl.ds(pl.multiple_of(core * width, 128), width)
    mine = pl.ds(pl.multiple_of(ROWS * c, 16), ROWS)
    local = []
    for n, (src, dst) in enumerate((
        (q_hbm.at[:, cols(c, 256)], qx.at[mine]),
        (k_hbm.at[:, cols(c, 256)], kx.at[mine]),
        (v_hbm.at[:, cols(c, 512)], vx.at[mine]),
        (g_hbm.at[:, cols(c, 512)], gx.at[mine]),
        (dec_hbm, dx.at[c]),
        (beta_hbm, bx.at[c]),
    )):
        local.append(pltpu.make_async_copy(src, dst, lsem.at[n + 1]))
        local[-1].start()

    pack = []
    for core in range(2):
        for n, (src, lo, width) in enumerate(((q_hbm, 0, 256), (k_hbm, 256, 256), (v_hbm, 512, 512))):
            pack.append(pltpu.make_async_copy(
                src.at[pl.ds(ROWS - HALO, HALO), pl.ds(core * width, width)],
                hb.at[core, :, pl.ds(lo, width)], hl.at[core, n],
            ))

    @pl.when(sends_halo)
    def _():
        for copy in pack:
            copy.start()

    @pl.when(chip == 0)
    def _():
        hx[...] = jnp.zeros_like(hx)

    @pl.when(~has_down)
    def _():
        s0buf[...] = jnp.zeros_like(s0buf)

    barrier = pltpu.get_barrier_semaphore()

    def signal(sem, **device):
        pl.semaphore_signal(sem, inc=1, device_id=device, device_id_type=MESH)

    def ring(k):
        return at(lax.rem(z + k + CHIPS, CHIPS))

    x_next, x_prev = lax.rem(x + 1, n_x), lax.rem(x + n_x - 1, n_x)
    signal(barrier, ctx=partner)
    signal(barrier, head=x_next)
    signal(barrier, head=x_prev)
    signal(barrier, ctx=ring(1))
    signal(barrier, ctx=ring(-1))

    @pl.when(has_prev)
    def _():
        signal(barrier, ctx=prev_tail)

    @pl.when(has_down)
    def _():
        signal(barrier, ctx=down)

    pl.semaphore_wait(barrier, 5 + jnp.where(sends_halo, 2, 0) + jnp.where(has_up, 1, 0))

    halo = []
    for core in range(2):
        halo.append(pltpu.make_async_remote_copy(
            hb.at[core], hx, hs.at[core], hr, device_id={"ctx": next_head + core}, device_id_type=MESH,
        ))

    @pl.when(sends_halo)
    def _():
        for copy in pack:
            copy.wait()
        for copy in halo:
            copy.start()

    trade = []
    for n, (src, dst) in enumerate((
        (dec_hbm, dx.at[c]),
        (beta_hbm, bx.at[c]),
        (k_hbm.at[:, cols(1 - c, 256)], kx.at[mine]),
        (q_hbm.at[:, cols(1 - c, 256)], qx.at[mine]),
        (v_hbm.at[:, cols(1 - c, 512)], vx.at[mine]),
        (g_hbm.at[:, cols(1 - c, 512)], gx.at[mine]),
    )):
        trade.append(pltpu.make_async_remote_copy(
            src, dst, xs.at[n], xr.at[n], device_id={"ctx": partner}, device_id_type=MESH,
        ))
        trade[-1].start()

    signal(told.at[0], ctx=ring(1))
    signal(told.at[1], ctx=ring(-1))

    first = chip * TOK
    sub = lax.broadcasted_iota(jnp.int32, (128, 128), 0)
    lane = lax.broadcasted_iota(jnp.int32, (128, 128), 1)
    lens = jnp.broadcast_to(docs_ref[...].astype(F32), (128, 128))
    starts_col = jnp.sum(jnp.where(lane < sub, lens, 0.0), axis=1, keepdims=True)
    starts_row = jnp.sum(jnp.where(sub < lane, lens.T, 0.0), axis=0, keepdims=True)
    pos_row = (first + lax.broadcasted_iota(jnp.int32, (128, TOK), 1)).astype(F32)
    seg_row = jnp.sum(jnp.where(starts_col <= pos_row, 1.0, 0.0), axis=0, keepdims=True)
    seg_prev = jnp.sum(jnp.where(starts_col <= (first - 1).astype(F32), 1.0, 0.0), axis=0, keepdims=True)
    seg_end = jnp.sum(jnp.where(starts_col <= (first + TOK - 1).astype(F32), 1.0, 0.0), axis=0, keepdims=True)
    pos_col = first + lax.broadcasted_iota(jnp.int32, (TOK, 128), 0)

    def seg_at(back):
        return jnp.sum(jnp.where(starts_row <= (pos_col - back).astype(F32), 1.0, 0.0), axis=1, keepdims=True)

    seg_col = seg_at(0)
    keeps = [None] + [(seg_at(j) == seg_col).astype(F32) for j in range(1, 4)]
    upper = (lax.broadcasted_iota(jnp.int32, (TOK, TOK), 0) <= lax.broadcasted_iota(jnp.int32, (TOK, TOK), 1)).astype(F32)
    halves = (slice(0, 128), slice(128, 256))
    quads = ((0, 0), (1, 0), (1, 1))
    same_doc = {}
    for r, s in quads:
        same = seg_col[halves[r]] == seg_row[:, halves[s]]
        same_doc[r, s] = same & (sub >= lane) if r == s else same

    for copy in local[4:]:
        copy.wait()
    for copy in trade[:2]:
        copy.wait_recv()

    decay = jnp.concatenate([dx[0], dx[1]], axis=1)
    log_gamma = -jax.nn.softplus(decay)
    cum8 = jnp.dot(log_gamma, upper, precision=lax.Precision.HIGHEST, preferred_element_type=F32)
    beta8 = jax.nn.sigmoid(jnp.concatenate([bx[0], bx[1]], axis=1))
    pick = lambda rows: jnp.where(c == 0, rows[:OWN], rows[OWN:])
    cum, beta = pick(cum8), pick(beta8)
    last = cum[:, TOK - 1:]
    to_end = jnp.where(seg_row == seg_end, jnp.exp(last - cum), 0.0)
    through = jnp.where(seg_end == seg_prev, jnp.exp(last), 0.0)
    by_token = jnp.concatenate([cum, beta], axis=0).T
    in_first = seg_col == seg_prev
    every = range(OWN)
    cum_cols = [by_token[:, i:i + 1] for i in every]
    beta_cols = [by_token[:, OWN + i:OWN + i + 1] for i in every]
    start_cols = [jnp.where(in_first, jnp.exp(cum_cols[i]), 0.0) for i in every]
    pairs, writes = [], []
    for i in every:
        pair, write = {}, {}
        for r, s in quads:
            diff = cum_cols[i][halves[r]] - cum[i:i + 1, halves[s]]
            pair[r, s] = jnp.exp(jnp.where(same_doc[r, s], diff, -1e30))
            write[r, s] = beta_cols[i][halves[r]] * pair[r, s]
            if r == s:
                write[r, s] = jnp.where(sub > lane, write[r, s], 0.0)
        pairs.append(pair)
        writes.append(write)

    pl.semaphore_wait(told.at[0], 1)
    pl.semaphore_wait(told.at[1], 1)
    signal(told.at[2], ctx=ring(2))
    signal(told.at[3], ctx=ring(-2))

    for copy in local[:4]:
        copy.wait()
    for copy in trade[2:5]:
        copy.wait_recv()

    xf[:HALO] = jnp.zeros((HALO, 1024), F32)
    for ref, lo, width in ((qx, 0, 256), (kx, 256, 256), (vx, 512, 512)):
        xf[HALO:, lo:lo + width] = ref[...].astype(F32)

    def activate(count, *parts):
        for w_ref, lo, width in parts:
            taps = w_ref[:, cols(c, width)]
            total = None
            for i in range(4):
                term = taps[i:i + 1] * xf[HALO - 3 + i:HALO - 3 + i + count, lo:lo + width]
                if i < 3:
                    term = term * keeps[3 - i][:count]
                total = term if total is None else total + term
            total = total * jax.nn.sigmoid(total)
            if lo < 512:
                for n in range(2):
                    head = total[:, n * DK:(n + 1) * DK]
                    norm = lax.rsqrt(jnp.sum(head * head, axis=-1, keepdims=True) + 1e-6)
                    act[:count, lo + n * DK:lo + (n + 1) * DK] = head * norm
            else:
                act[:count, lo:lo + width] = total

    of_q, of_k, of_v = (cq_ref, 0, 256), (ck_ref, 256, 256), (cv_ref, 512, 512)
    activate(TOK, of_k, of_v)

    @pl.when(has_prev)
    def _():
        halo[0].wait_recv()

    xf[:HALO] = hx[...].astype(F32)
    activate(8, of_k, of_v)

    def lanes(size, height):
        where = lax.broadcasted_iota(jnp.int32, (height, 128), 1) // size
        return [(where == b).astype(BF16) for b in range(128 // size)]

    def expand(packed, size, masks, rows):
        zero = jnp.zeros((size, 128), BF16)
        out = []
        for b in range(TOK // size):
            src = rows(b)
            if src is None:
                out.append(jnp.concatenate([zero, zero], axis=1))
                continue
            half, inner = src * size // 128, src % (128 // size)
            piece = packed[:, halves[half]] * masks[inner]
            out.append(jnp.concatenate([piece, zero] if half == 0 else [zero, piece], axis=1))
        return jnp.concatenate(out, axis=0)

    def gather(low, size, masks, row_block, lane_block, count):
        both = []
        for half in range(2):
            total = None
            for p in range(count // 2):
                r, s = row_block(p), lane_block(p)
                piece = low[half, half][r * size:(r + 1) * size] * masks[s]
                total = piece if total is None else total + piece
            both.append(total)
        return jnp.concatenate(both, axis=1)

    kfs = [act[:, 256 + n * DK:256 + (n + 1) * DK] for n in range(2)]
    kbs = [kf.astype(BF16) for kf in kfs]
    k_ts = [kf.T for kf in kfs]
    k_tbs = [k_t.astype(BF16) for k_t in k_ts]
    grams = [dot(kbs[n], k_tbs[n]) for n in range(2)]
    lows = []
    for i in every:
        low = {}
        for r, s in quads:
            low[r, s] = (grams[i // 2][halves[r], halves[s]] * writes[i][r, s]).astype(BF16)
        lows.append(low)

    m16 = lanes(16, 16)
    diag = lambda b: b
    eye16 = (lax.broadcasted_iota(jnp.int32, (16, TOK), 0) == lax.broadcasted_iota(jnp.int32, (16, TOK), 1) % 16).astype(F32)
    n1 = [-gather(lows[i], 16, m16, lambda p: p, lambda p: p, 16) for i in every]
    t = [eye16 + n1[i].astype(F32) for i in every]
    n2 = [dot(n1[i], expand(n1[i], 16, m16, diag)).astype(BF16) for i in every]
    power = n2
    for last_step in (False, False, True):
        wide = [expand(power[i], 16, m16, diag) for i in every]
        if last_step:
            t = [t[i] + dot(t[i].astype(BF16), wide[i]) for i in every]
        else:
            both = [dot(jnp.concatenate([power[i], t[i].astype(BF16)], axis=0), wide[i]) for i in every]
            power = [both[i][:16].astype(BF16) for i in every]
            t = [t[i] + both[i][16:] for i in every]

    for size in (16, 32, 64):
        masks = lanes(size, size)
        even = (lax.broadcasted_iota(jnp.int32, (size, TOK), 1) // size) % 2 == 0
        tb = [t[i].astype(BF16) for i in every]
        edge = [gather(lows[i], size, masks, lambda p: 2 * p + 1, lambda p: 2 * p, TOK // size // 2) for i in every]
        y = [dot(edge[i], expand(tb[i], size, masks, lambda b: b if b % 2 == 0 else None)).astype(BF16) for i in every]
        below = [dot(tb[i], expand(y[i], size, masks, lambda b: b - 1 if b % 2 else None)) for i in every]
        t = [jnp.concatenate([jnp.where(even, t[i], 0.0), jnp.where(even, -below[i], t[i])], axis=0) for i in every]

    rhs = []
    for i in every:
        v = act[:, 512 + i * DK:512 + (i + 1) * DK]
        rhs.append((beta_cols[i] * v, (beta_cols[i] * start_cols[i]) * kfs[i // 2]))
    tb = [t[i].astype(BF16) for i in every]
    rhs = [jnp.concatenate(rhs[i], axis=1) for i in every]
    uw_top = [dot(tb[i][:, :128], rhs[i][:128].astype(BF16)).astype(BF16) for i in every]
    rest = [(rhs[i][128:] - dot(lows[i][1, 0], uw_top[i])).astype(BF16) for i in every]
    uw = [jnp.concatenate([uw_top[i], dot(tb[i][:, 128:], rest[i]).astype(BF16)], axis=0) for i in every]
    kuw = [fine_dot(k_ts[i // 2] * to_end[i:i + 1], uw[i]) for i in every]
    eye = (sub == lane).astype(F32)
    for i in every:
        mb[i, :, :DK] = (through[i:i + 1] * eye - kuw[i][:, DK:]).astype(BF16)
        mb[i, :, DK:] = kuw[i][:, :DK].astype(BF16)

    pl.semaphore_wait(told.at[2], 1)
    pl.semaphore_wait(told.at[3], 1)
    sends = []
    for i in every:
        owner = OWN * c + i
        sends.append((owner, pltpu.make_async_remote_copy(
            mb.at[i], rbuf.at[z], as_.at[i], ar.at[z], device_id={"ctx": at(owner)}, device_id_type=MESH,
        )))
    for owner, send in sends:
        @pl.when(z != owner)
        def _():
            send.start()

    @pl.when(own)
    def _():
        rbuf[z] = mb[head_at]

    activate(TOK, of_q)
    qfs = [act[:, n * DK:(n + 1) * DK] for n in range(2)]
    scores = [dot(qfs[n].astype(BF16), k_tbs[n]) for n in range(2)]
    for i in every:
        inside = {q: scores[i // 2][halves[q[0]], halves[q[1]]] * pairs[i][q] for q in quads}
        top = fine_dot(inside[0, 0], uw_top[i])
        bottom = fine_dot(jnp.concatenate([inside[1, 0], inside[1, 1]], axis=1), uw[i])
        q_start = qfs[i // 2] * start_cols[i]
        oloc[i, :128] = top[:, :DK]
        oloc[i, 128:] = bottom[:, :DK]
        qeff[i, :128] = (q_start[:128] - top[:, DK:]).astype(BF16)
        qeff[i, 128:] = (q_start[128:] - bottom[:, DK:]).astype(BF16)
    trade[5].wait_recv()
    gate = gx[...].astype(F32)
    gated[...] = gate * jax.nn.sigmoid(gate) * jnp.concatenate([gain_ref[...]] * OWN, axis=1)

    mine_at = jnp.where(own, head_at, 0)
    back = []
    for k in range(1, CHIPS):
        back.append(pltpu.make_async_remote_copy(
            sout.at[k], sbuf.at[mine_at], ss.at[k], sr.at[mine_at], device_id={"ctx": ring(k)}, device_id_type=MESH,
        ))
    ahead = pltpu.make_async_remote_copy(q8, s0buf, ys, yr, device_id={"ctx": up}, device_id_type=MESH)

    @pl.when(own)
    def _():
        for k in range(1, CHIPS):
            j = lax.rem(z + k, CHIPS)
            pltpu.make_async_remote_copy(
                mb.at[0], rbuf.at[j], as_.at[0], ar.at[j], device_id={"ctx": ring(k)}, device_id_type=MESH,
            ).wait_recv()

        def then(later, earlier):
            joined = dot(later[:, :DK], earlier)
            return jnp.concatenate([joined[:, :DK], joined[:, DK:] + later[:, DK:].astype(F32)], axis=1).astype(BF16)

        one = [rbuf[j] for j in range(CHIPS)]
        two = [then(one[2 * j + 1], one[2 * j]) for j in range(4)]
        four = [then(two[1], two[0]), then(two[3], two[2])]
        q8[...] = (dot(four[1][:, :DK], four[0][:, DK:]) + four[1][:, DK:].astype(F32)).astype(BF16)

        @pl.when(has_up)
        def _():
            ahead.start()

        six = then(two[2], four[0])
        start = jnp.concatenate([eye, jnp.zeros((DK, DK), F32)], axis=1).astype(BF16)
        for j, value in enumerate((
            start, one[0], two[0], then(one[2], two[0]), four[0], then(one[4], four[0]), six, then(one[6], six),
        )):
            pre[j] = value

        @pl.when(has_down)
        def _():
            ahead.wait_recv()

        s0 = s0buf[...]
        for k in (4, 3, 5, 2, 6, 1, 7, 0):
            step = pre[lax.rem(z + k, CHIPS)]
            state = (dot(step[:, :DK], s0) + step[:, DK:].astype(F32)).astype(BF16)
            if k:
                sout[k] = state
                back[k - 1].start()
            else:
                sbuf[head_at] = state

    for i in every:
        @pl.when(z != OWN * c + i)
        def _():
            pltpu.make_async_remote_copy(
                sout.at[0], sbuf.at[i], ss.at[0], sr.at[i], device_id={"ctx": partner}, device_id_type=MESH,
            ).wait_recv()
    theirs = pl.ds(pl.multiple_of(ROWS * (1 - c), 16), ROWS)
    swap = pltpu.make_async_remote_copy(
        mx.at[theirs], mixfull, ms, mr, device_id={"ctx": partner}, device_id_type=MESH,
    )
    for tokens in (theirs, mine):
        for i in every:
            o = oloc[i, tokens] + dot(qeff[i, tokens], sbuf[i])
            normed = o * lax.rsqrt(jnp.mean(o * o, axis=-1, keepdims=True) + 1e-6)
            mx[tokens, i * DK:(i + 1) * DK] = (normed * gated[tokens, i * DK:(i + 1) * DK]).astype(BF16)
        if tokens is theirs:
            swap.start()
    w_copy.wait()

    half = OWN * DK
    rows = lambda core: pl.ds(pl.multiple_of(core * half, 128), half)
    width = w_vm.shape[1] // 4
    mixed = mx[mine]
    order = (2, 1, 3, 0)
    for k in order:
        own_part[k] = dot(mixed, w_vm[rows(c), cols(lax.rem(x + k, n_x), width)])
    swap.wait_recv()
    mixed = mixfull[...]

    def part(k):
        block = cols(lax.rem(x + k, n_x), width)
        return (own_part[k] + dot(mixed, w_vm[rows(1 - c), block])).astype(BF16)

    sent = []

    def pass_on(n, src, dst, to):
        sent.append(pltpu.make_async_remote_copy(
            src, dst, ps.at[n], pr.at[n], device_id={"head": to}, device_id_type=MESH,
        ))
        sent[-1].start()

    piece = ROWS // 4
    rows_of = [pl.ds(n * piece, piece) for n in range(4)]
    early, late = pl.ds(0, ROWS // 2), pl.ds(ROWS // 2, ROWS // 2)
    sendp[1] = part(2)
    for n in (0, 2, 1, 3):
        pass_on(n, sendp.at[1, rows_of[n]], via.at[n], x_next if n < 2 else x_prev)
    sendp[0] = part(1)
    pass_on(4, sendp.at[0, late], recvp.at[0, late], x_next)
    sendp[2] = part(3)
    pass_on(5, sendp.at[2, early], recvp.at[1, early], x_prev)
    total = part(0).astype(F32)
    for at_sent, n in enumerate((0, 2, 1, 3)):
        side = 0 if n < 2 else 1
        sent[at_sent].wait_recv()
        joined[n] = (sendp[2 * side, rows_of[n]].astype(F32) + via[n].astype(F32)).astype(BF16)
        pass_on(6 + n, joined.at[n], recvp.at[side, rows_of[n]], x_prev if side else x_next)
    for copy in sent[4:]:
        copy.wait_recv()
    out_ref[...] = (total + recvp[0].astype(F32) + recvp[1].astype(F32)).T.astype(BF16)

    for copy in trade + [swap] + sent:
        copy.wait_send()

    @pl.when(sends_halo)
    def _():
        for copy in halo:
            copy.wait_send()

    for owner, send in sends:
        @pl.when(z != owner)
        def _():
            send.wait_send()

    @pl.when(own & has_up)
    def _():
        ahead.wait_send()

    @pl.when(own)
    def _():
        for copy in back:
            copy.wait_send()


def body(
    query_in, key_in, value_in, gate_in, conv_query, conv_key, conv_value,
    decay_in, beta_in, norm_gain, doc_lengths, out_weight,
):
    anywhere, vmem = pl.BlockSpec(memory_space=pl.ANY), pl.BlockSpec(memory_space=pltpu.VMEM)
    dma = pltpu.SemaphoreType.DMA
    features = out_weight.shape[1] // 4
    return pl.pallas_call(
        kernel,
        out_shape=jax.ShapeDtypeStruct((features, ROWS), BF16),
        in_specs=[anywhere] * 7 + [vmem] * 5,
        out_specs=vmem,
        scratch_shapes=[
            pltpu.VMEM((TOK, 256), BF16),
            pltpu.VMEM((TOK, 256), BF16),
            pltpu.VMEM((TOK, 512), BF16),
            pltpu.VMEM((TOK, 512), BF16),
            pltpu.VMEM((2, 8, ROWS), F32),
            pltpu.VMEM((2, 8, ROWS), F32),
            pltpu.VMEM((2, HALO, 1024), BF16),
            pltpu.VMEM((HALO, 1024), BF16),
            pltpu.VMEM((HALO + TOK, 1024), F32),
            pltpu.VMEM((TOK, 1024), F32),
            pltpu.VMEM(out_weight.shape, BF16),
            pltpu.VMEM((OWN, DK, 2 * DK), BF16),
            pltpu.VMEM((OWN, TOK, DK), BF16),
            pltpu.VMEM((OWN, TOK, DK), F32),
            pltpu.VMEM((CHIPS, DK, 2 * DK), BF16),
            pltpu.VMEM((CHIPS, DK, 2 * DK), BF16),
            pltpu.VMEM((DK, DK), BF16),
            pltpu.VMEM((DK, DK), BF16),
            pltpu.VMEM((CHIPS, DK, DK), BF16),
            pltpu.VMEM((OWN, DK, DK), BF16),
            pltpu.VMEM((TOK, OWN * DK), F32),
            pltpu.VMEM((TOK, OWN * DK), BF16),
            pltpu.VMEM((ROWS, OWN * DK), BF16),
            pltpu.VMEM((4, ROWS, features), F32),
            pltpu.VMEM((3, ROWS, features), BF16),
            pltpu.VMEM((4, ROWS // 4, features), BF16),
            pltpu.VMEM((4, ROWS // 4, features), BF16),
            pltpu.VMEM((2, ROWS, features), BF16),
            dma((7,)), dma((6,)), dma((6,)), dma((2, 3)), dma((2,)), dma,
            dma((OWN,)), dma((CHIPS,)), dma, dma, dma((CHIPS,)), dma((OWN,)),
            dma, dma, dma((10,)), dma((10,)), pltpu.SemaphoreType.REGULAR((4,)),
        ],
        compiler_params=pltpu.CompilerParams(
            collective_id=0, has_side_effects=True, vmem_limit_bytes=56 << 20
        ),
        name="mixer",
    )(
        query_in, key_in, value_in, gate_in, decay_in, beta_in, out_weight,
        conv_query, conv_key, conv_value, doc_lengths.reshape(1, -1), norm_gain.reshape(1, -1),
    )


def solution(mesh):
    return jax.shard_map(
        body,
        mesh=mesh,
        in_specs=(
            P("ctx", "head"), P("ctx", "head"), P("ctx", "head"), P("ctx", "head"),
            P(None, "head"), P(None, "head"), P(None, "head"),
            P("head", "ctx"), P("head", "ctx"), P(), P(), P("head", None),
        ),
        out_specs=P("head", "ctx"),
        check_vma=False,
    )
```
